512 devices in a mesh: kv: 4 (over x), wide: 128 (over y, z, core).
Axes of the slice: x: 4, y: 8, z: 8, core: 2. Of those that a mesh axis runs over, the one named last changes fastest.
Arguments:
- stream_in: bfloat16 [256, 4, 2560], P('wide', None, 'kv'), may hold values from -8 to 8
- queries: bfloat16 [256, 4, 2560], P('wide', None, 'kv'), may hold values from -2.5 to 2.5
- new_kv: bfloat16 [256, 4, 2, 512], P('wide', None, None, 'kv'), may hold values from -2.5 to 2.5
- cache_keys: bfloat16 [4, 2048, 128, 128], P('kv', 'wide'), may hold values from -2.5 to 2.5
- cache_values: bfloat16 [4, 2048, 128, 128], P('kv', 'wide'), may hold values from -2.5 to 2.5
- lengths: int32 [32], replicated, may hold values from 1 to 4096, as said below
- page_table: int32 [32, 32], replicated, may hold values from -1 to 2047, as said below
- parents: int32 [256, 3], replicated, may hold values from 0 to 7
- routes: int32 [256, 4, 6], P('wide'), may hold values from 0 to 63, all different within a row; in each aligned block of 8 rows (0 to 7, 8 to 15, ..., all dimensions but the last counted through in order) at most 2 rows name the same one
- norm_gain: float32 [2560], replicated, may hold values from 0.5 to 1.5
- router: bfloat16 [2560, 64], replicated, may hold values from -0.01965332 to 0.01965332
- gate_w: bfloat16 [128, 2560, 768], P('wide', None, 'kv'), may hold values from -0.125 to 0.125
- up_w: bfloat16 [128, 2560, 768], P('wide', None, 'kv'), may hold values from -0.125 to 0.125
- down_w: bfloat16 [128, 768, 2560], P('wide', 'kv'), may hold values from -0.15625 to 0.15625
Outputs:
- stream_out: bfloat16 [256, 4, 2560], P('wide', None, 'kv')
The draws below stay inside these ranges and needn't reach their ends.
Inputs may be any that keep to these rules, and one draw needn't show every extreme that they name: `lengths`: one group has exactly 4096 positions. `page_table`: entry [g, b] is the slot (index of wide times 16 plus the local slot) holding positions b * 128 to b * 128 + 127 of group g when b * 128 < lengths[g], and -1 otherwise; no slot is named twice; every slot of some index of wide is named. `parents`: entry [t, j] is a beam of t's own group. `routes`: within the rows of one index of wide (2 beams times 4 steps) no expert is named by more than 2 rows.
All inputs are finite; a program needn't handle non-finite values.
Results may differ from the reference program's by a relative error of at most 0.012.
Values may be sent and summed in bfloat16 or wider, within the bound.
A program may use at most 64 MiB of HBM per device.

```python
import math
import jax
import jax.numpy as jnp
import numpy as np
from jax import lax

D = 2560
QH = 20
KVH = 4
HD = 128
E = 64
FF = 1536
TOP = 6
BEAMS = 8
STEPS = 4
STEP_TOK = 2
BLK = 128
MAXLEN = 4096
MAXB = 32
SLOTS_DEV = 16
SLOTS_ALL = 2048
GROUPS = 32
TOKENS = 256
MOST = 2
N_WIDE = 128


def cache_layout(key):
    subkeys = jax.random.split(jax.random.fold_in(key, 41), 5)
    exponents = jax.random.randint(subkeys[0], (GROUPS,), 0, 14)
    span_cap = jnp.minimum(jnp.left_shift(jnp.ones((GROUPS,), jnp.int32), exponents), MAXLEN)
    raw_draw = jax.random.randint(subkeys[1], (GROUPS,), 0, MAXLEN)
    group_sizes = 1 + raw_draw % span_cap
    longest = jax.random.randint(subkeys[2], (), 0, GROUPS)
    group_sizes = jnp.where(jnp.arange(GROUPS) == longest, MAXLEN, group_sizes)
    block_used = jnp.arange(MAXB)[None, :] * BLK < group_sizes[:, None]
    flat_used = block_used.reshape(-1)
    used_rank = jnp.cumsum(flat_used.astype(jnp.int32)) - 1
    shuffle = jax.random.permutation(subkeys[3], SLOTS_ALL)
    full_device = jax.random.randint(subkeys[4], (), 0, SLOTS_ALL // SLOTS_DEV)
    slot_ids = jnp.arange(SLOTS_ALL)
    slot_score = shuffle + jnp.where(slot_ids // SLOTS_DEV == full_device, 0, SLOTS_ALL)
    slot_order = jnp.argsort(slot_score, stable=True)
    page_rows = jnp.where(flat_used, slot_order[jnp.maximum(used_rank, 0)], -1)
    return (group_sizes.astype(jnp.int32), page_rows.reshape(GROUPS, MAXB).astype(jnp.int32))


def draw_lengths(key, part):
    return cache_layout(key)[0]


def draw_page_table(key, part):
    return cache_layout(key)[1]


def draw_stream_in(key, part):
    subkeys = jax.random.split(jax.random.fold_in(key, 5), 1)
    normal_base = jax.random.normal(subkeys[0], (TOKENS, STEPS, D), jnp.float32)
    return jnp.clip(normal_base, -8.0, 8.0).astype(jnp.bfloat16)


def place_ends(result, own_key, smallest, largest):
    longest = result.shape.index(max(result.shape))
    spots = []
    for shift in (0, 1):
        where = [jax.random.randint(jax.random.fold_in(own_key, axis), (), 0, length) for axis, length in enumerate(result.shape)]
        where[longest] = (where[longest] + shift) % result.shape[longest]
        spots.append(tuple(where))
    return result.at[spots[0]].set(smallest).at[spots[1]].set(largest)


def shard_levels(own_key, extent, pieces, smallest, largest):
    def one(axis_at, parts):
        draws = jax.random.uniform(jax.random.fold_in(jax.random.fold_in(own_key, 6), axis_at), (parts,), jnp.float32, smallest / len(pieces), largest / len(pieces))
        return jnp.repeat(jnp.exp(draws), extent[axis_at] // parts).reshape((-1,) + (1,) * (len(extent) - axis_at - 1))

    loudness = one(*pieces[0])
    for cut in pieces[1:]:
        loudness = loudness * one(*cut)
    return loudness


def routed_block(own_key, own, number, rows, amount, top, most, slope):
    sequence = jax.random.permutation(own_key, amount)
    heavy_load, usual = shares(amount, rows * top, most, slope, True), shares(amount, rows * top, most, slope, False)
    places = jnp.arange(amount)

    def named(sizes, offset_by):
        used = int((sizes > 0).sum())
        fixed = max(1, used // 4)
        shifted = fixed + (places - fixed + offset_by * (used - fixed)) % max(1, amount - fixed)
        return jnp.zeros((amount,), jnp.int32).at[sequence[jnp.where(places < fixed, places, shifted)]].set(jnp.asarray(sizes, jnp.int32))

    sizes = jnp.where(number % 4 == 0, named(heavy_load, number // 4), named(usual, number - number // 4 - 1))
    mixed = jax.random.permutation(jax.random.fold_in(own, 3), amount)
    donor, sink = mixed[0:amount // 2 * 2:2], mixed[1:amount // 2 * 2:2]
    slack = jnp.minimum(sizes[donor] - 1, most - sizes[sink]) // 2
    slack = jnp.where((donor == sequence[0]) | (sink == sequence[0]) | (sizes[sink] == 0), 0, jnp.maximum(slack, 0))
    shifted = jax.random.randint(jax.random.fold_in(own, 4), (amount // 2,), 0, 1 << 20) % (slack + 1)
    sizes = sizes.at[donor].add(-shifted).at[sink].add(shifted)
    members = jnp.searchsorted(jnp.cumsum(sizes), jnp.arange(rows * top), side="right").astype(jnp.int32)
    grid = members.reshape(top, rows).T
    grid = grid[jax.random.permutation(jax.random.fold_in(own, 1), rows)]
    offset_by = jax.random.randint(jax.random.fold_in(own, 2), (rows, 1), 0, top)
    return jnp.take_along_axis(grid, (jnp.arange(top)[None, :] + offset_by) % top, axis=1)


def shares(amount, total, reach, skew, full):
    weights = [(1 << 20) // math.isqrt(grade ** skew) + 1 for grade in range(1, amount + 1)]
    largest = reach if full else min(reach, max(-(-total // amount), total * weights[0] // sum(weights)))
    least = 1 if total - largest >= amount - 1 else 0
    counts, rest = [largest] + [least] * (amount - 1), total - largest - least * (amount - 1)
    while rest > 0:
        free = [i for i in range(1, amount) if counts[i] < largest] or [i for i in range(1, amount) if counts[i] < reach]
        whole, left = sum([weights[i] for i in free]), rest
        for i in free:
            addition = min(reach - counts[i], max(1, left * weights[i] // whole), rest)
            counts[i] = counts[i] + addition
            rest = rest - addition
    return np.array(counts)


def centred(rng, extent, spread, limit, cuts=(), kind=jnp.bfloat16):
    drawn = spread * jax.random.normal(rng, extent, jnp.float32)
    if cuts:
        drawn = drawn * shard_levels(rng, extent, cuts, -0.22, 0.18)
    return jnp.clip(drawn, -limit, limit).astype(kind)


def setup_inputs(seed: int = 0) -> dict:
    seeds = jax.random.split(jax.random.key(seed), 15)
    stream_in = draw_stream_in(jax.random.fold_in(seeds[14], 71), 0)
    queries = centred(seeds[1], (TOKENS, STEPS, QH * HD), 1.0, 2.5, ((0, 128), (2, 4)))
    new_kv = centred(seeds[2], (TOKENS, STEPS, 2, KVH * HD), 1.0, 2.5, ((0, 128), (3, 4)))
    cache_keys = centred(seeds[3], (KVH, SLOTS_ALL, BLK, HD), 1.0, 2.5, ((0, 4), (1, 128)))
    cache_values = centred(seeds[4], (KVH, SLOTS_ALL, BLK, HD), 1.0, 2.5, ((0, 4), (1, 128)))
    lengths = draw_lengths(jax.random.fold_in(seeds[14], 71), 0)
    page_table = draw_page_table(jax.random.fold_in(seeds[14], 71), 0)
    parents = place_ends(jax.random.randint(seeds[7], (TOKENS, STEPS - 1), 0, BEAMS), jax.random.fold_in(seeds[7], 1), 0, BEAMS - 1).astype(jnp.int32)
    routes_keys = jax.random.split(jax.random.fold_in(seeds[8], 1), TOKENS * STEPS // (STEPS * STEP_TOK))
    routes_turns = jax.random.permutation(jax.random.fold_in(seeds[8], 3), TOKENS * STEPS // (STEPS * STEP_TOK))
    routes = jax.vmap(lambda own, number: routed_block(jax.random.fold_in(seeds[8], 2), own, number, STEPS * STEP_TOK, E, TOP, MOST, 2))(routes_keys, routes_turns).reshape((TOKENS, STEPS, TOP))
    norm_gain = jnp.clip(1.0 + 0.1 * jax.random.normal(seeds[9], (D,), jnp.float32), 0.5, 1.5)
    router = jnp.clip(jax.random.uniform(seeds[10], (D, E), jnp.float32, -0.01965332, 0.01965332), -0.01965332, 0.01965332).astype(jnp.bfloat16)
    gate_w = centred(seeds[11], (2 * E, D, FF // 2), D ** -0.5, 0.125, ((0, 128), (2, 4)))
    up_w = centred(seeds[12], (2 * E, D, FF // 2), D ** -0.5, 0.125, ((0, 128), (2, 4)))
    down_w = centred(seeds[13], (2 * E, FF // 2, D), FF ** -0.5, 0.15625, ((0, 128), (1, 4)))
    return dict(stream_in=stream_in, queries=queries, new_kv=new_kv, cache_keys=cache_keys, cache_values=cache_values, lengths=lengths, page_table=page_table, parents=parents, routes=routes, norm_gain=norm_gain, router=router, gate_w=gate_w, up_w=up_w, down_w=down_w)


def chain_tokens(parents):
    tokens = jnp.arange(TOKENS, dtype=jnp.int32)
    group_base = tokens // BEAMS * BEAMS
    chain_table = []
    for step_now in range(STEPS):
        columns = [tokens] * STEPS
        current = tokens
        for earlier in range(step_now, 0, -1):
            current = (group_base + parents[current, earlier - 1]).astype(jnp.int32)
            columns[earlier - 1] = current
        chain_table.append(jnp.stack(columns, axis=1))
    return jnp.stack(chain_table, axis=1)

def reference(stream_in, queries, new_kv, cache_keys, cache_values, lengths, page_table, parents, routes, norm_gain, router, gate_w, up_w, down_w):
    score_scale = 1.0 / math.sqrt(HD)
    head_ratio = QH // KVH
    chains = chain_tokens(parents)
    history = new_kv[chains, jnp.arange(STEPS, dtype=jnp.int32)[None, None, :]]
    causal = (jnp.arange(STEPS)[None, :] <= jnp.arange(STEPS)[:, None]).astype(jnp.float32)
    positions = jnp.arange(MAXLEN, dtype=jnp.int32)

    def one_group(group_id):
        first_token = (group_id * BEAMS).astype(jnp.int32)
        group_queries = lax.dynamic_slice_in_dim(queries, first_token, BEAMS, 0).astype(jnp.float32)
        group_queries = group_queries.reshape(BEAMS, STEPS, KVH, head_ratio, HD)
        page_rows = jnp.maximum(page_table[group_id], 0)
        block_keys = cache_keys[:, page_rows].reshape(KVH, MAXLEN, HD).astype(jnp.float32)
        block_values = cache_values[:, page_rows].reshape(KVH, MAXLEN, HD).astype(jnp.float32)
        valid_mask = (positions < lengths[group_id]).astype(jnp.float32)
        scores = jnp.einsum('bskrd,kpd->bskrp', group_queries, block_keys)
        weights = (jnp.exp(scores * score_scale) * valid_mask).astype(jnp.bfloat16)
        weights = lax.optimization_barrier(weights).astype(jnp.float32)
        numerator = jnp.einsum('bskrp,kpd->bskrd', weights, block_values)
        denominator = lax.optimization_barrier(jnp.sum(weights, axis=-1))
        past_rows = lax.dynamic_slice_in_dim(history, first_token, BEAMS, 0).astype(jnp.float32)
        tail_keys = past_rows[:, :, :, 0].reshape(BEAMS, STEPS, STEPS, KVH, HD)
        tail_values = past_rows[:, :, :, 1].reshape(BEAMS, STEPS, STEPS, KVH, HD)
        tail_scores = jnp.einsum('bskrd,bsjkd->bskrj', group_queries, tail_keys)
        tail_weights = (jnp.exp(tail_scores * score_scale) * causal[None, :, None, None, :]).astype(jnp.bfloat16)
        tail_weights = lax.optimization_barrier(tail_weights).astype(jnp.float32)
        numerator = numerator + jnp.einsum('bskrj,bsjkd->bskrd', tail_weights, tail_values)
        denominator = denominator + lax.optimization_barrier(jnp.sum(tail_weights, axis=-1))
        attended = (numerator / denominator[..., None]).astype(jnp.bfloat16)
        return attended.reshape(BEAMS, STEPS, QH * HD)
    attended = lax.map(one_group, jnp.arange(GROUPS, dtype=jnp.int32)).reshape(TOKENS, STEPS, D)
    residual = (stream_in.astype(jnp.float32) + attended.astype(jnp.float32)).astype(jnp.bfloat16)
    row_count = TOKENS * STEPS
    token_rows = residual.reshape(row_count, D).astype(jnp.float32)
    mean_square = lax.optimization_barrier(jnp.mean(token_rows * token_rows, axis=1, keepdims=True))
    normed = (token_rows * lax.rsqrt(mean_square + 1e-06) * norm_gain[None, :]).astype(jnp.bfloat16)
    logits = jnp.dot(normed, router, preferred_element_type=jnp.float32)
    routed = routes.reshape(row_count, TOP)
    chosen = jnp.take_along_axis(logits, routed, axis=1)
    raised = jnp.exp(chosen)
    gate_share = raised / lax.optimization_barrier(jnp.sum(raised, axis=1, keepdims=True))
    capacity = N_WIDE * MOST
    padded = jnp.concatenate([normed, jnp.zeros((1, D), jnp.bfloat16)], axis=0)

    def add_expert(summed, expert):
        expert_hit = routed == expert
        weight = lax.optimization_barrier(jnp.sum(jnp.where(expert_hit, gate_share, 0.0), axis=1))
        expert_used = jnp.any(expert_hit, axis=1)
        row_index = jnp.nonzero(expert_used, size=capacity, fill_value=row_count)[0].astype(jnp.int32)
        expert_rows = padded[row_index]
        gate_full = jnp.concatenate([gate_w[2 * expert], gate_w[2 * expert + 1]], axis=1)
        up_full = jnp.concatenate([up_w[2 * expert], up_w[2 * expert + 1]], axis=1)
        down_full = jnp.concatenate([down_w[2 * expert], down_w[2 * expert + 1]], axis=0)
        gate_out = jnp.dot(expert_rows, gate_full, preferred_element_type=jnp.float32)
        up_out = jnp.dot(expert_rows, up_full, preferred_element_type=jnp.float32)
        hidden = (jax.nn.silu(gate_out) * up_out).astype(jnp.bfloat16)
        expert_out = jnp.dot(hidden, down_full, preferred_element_type=jnp.float32)
        weight_pad = jnp.concatenate([weight, jnp.zeros((1,), jnp.float32)])
        return (summed.at[row_index].add(expert_out * weight_pad[row_index][:, None]), None)
    summed, unused = lax.scan(add_expert, jnp.zeros((row_count + 1, D), jnp.float32), jnp.arange(E, dtype=jnp.int32))
    mixed_rows = (residual.reshape(row_count, D).astype(jnp.float32) + summed[:row_count]).astype(jnp.bfloat16)
    return mixed_rows.reshape(TOKENS, STEPS, D)
```

```python
import functools
import math

import jax
import jax.numpy as jnp
from jax import lax
from jax.experimental import pallas as pl
from jax.experimental.pallas import tpu as pltpu
from jax.sharding import PartitionSpec as P

MESH = pl.DeviceIdType.MESH
HD = 128
BEAMS = 8
BLK = 128
MOST = 2
F32 = jnp.float32
BF16 = jnp.bfloat16


def far_first(n):
    order = sorted(range(1, n), key=lambda d: -min(d, n - d))
    return order


def near_first(n):
    return sorted(range(1, n), key=lambda d: min(d, n - d))


def rcopy(src, dst, send_sem, recv_sem, device):
    return pltpu.make_async_remote_copy(
        src_ref=src,
        dst_ref=dst,
        send_sem=send_sem,
        recv_sem=recv_sem,
        device_id=device,
        device_id_type=MESH,
    )


def dot(x, y):
    return jnp.dot(x, y, preferred_element_type=F32)


def iota(shape, axis):
    return lax.broadcasted_iota(jnp.int32, shape, axis)


def kernel(
    n,
    kv_count,
    heads,
    stream_ref,
    query_ref,
    newkv_ref,
    keys_hbm,
    values_hbm,
    lengths_ref,
    table_ref,
    parents_ref,
    routes_ref,
    gain_ref,
    router_hbm,
    gate_hbm,
    up_hbm,
    down_hbm,
    out_ref,
    keys,
    values,
    router,
    gate,
    up,
    down,
    load_sem,
    qfull,
    kvgroup,
    q_sems,
    slot_group,
    slot_limit,
    slot_prev,
    group_last,
    sums,
    part,
    sibling_part,
    core_sum,
    b_parts,
    b_sum,
    a_parts,
    part_sems,
    resid,
    resid_all,
    x_sems,
    outgoing,
    mid_rows,
    mid_perm,
    rows,
    row_sems,
    expert_part,
    expert_sib,
    x_send,
    x_recv,
    back_a,
    back_mid,
    back_perm,
    back_rows,
    back_sems,
):
    kv = lax.axis_index("kv")
    w = lax.axis_index("wide")
    c = w % 2
    z = (w // 2) % n
    y = w // (2 * n)
    a = z + c * (y - z)
    b = y + c * (z - y)
    stride_a = 2 + c * (2 * n - 2)
    stride_b = 2 * n - c * (2 * n - 2)
    sib = {"wide": w + 1 - 2 * c}
    width = heads * HD
    row_count = query_ref.shape[0]
    slots = keys.shape[0]
    groups = lengths_ref.shape[0]
    blocks = table_ref.shape[1]
    steps = parents_ref.shape[1] + 1
    top = routes_ref.shape[1]
    scale = 1.0 / math.sqrt(HD)

    def dev_a(j):
        return {"wide": w + (j - a) * stride_a}

    def dev_b(j):
        return {"wide": w + (j - b) * stride_b}

    def dev_x(j):
        return {"kv": j}

    group_first = w // 4 * 4
    group_place = w % 4

    loads = [
        pltpu.make_async_copy(src, dst, load_sem.at[i])
        for i, (src, dst) in enumerate(
            [
                (keys_hbm.at[0], keys),
                (values_hbm.at[0], values),
                (router_hbm, router),
                (gate_hbm.at[0], gate),
                (up_hbm.at[0], up),
                (down_hbm.at[0], down),
            ]
        )
    ]
    own_query = pltpu.make_async_copy(query_ref, qfull.at[c, b, a], load_sem.at[6])
    own_kv = pltpu.make_async_copy(newkv_ref, kvgroup.at[group_place], load_sem.at[7])
    own_query.start()
    own_kv.start()
    for load in loads:
        load.start()

    barrier = pltpu.get_barrier_semaphore()
    greeted = 0
    for d in far_first(n):
        for device in (dev_a((a + d) % n), dev_b((b + d) % n)):
            pl.semaphore_signal(barrier, inc=1, device_id=device, device_id_type=MESH)
            greeted += 1
    for d in range(1, kv_count):
        pl.semaphore_signal(
            barrier, inc=1, device_id=dev_x((kv + d) % kv_count), device_id_type=MESH
        )
        greeted += 1
    for d in range(1, 4):
        pl.semaphore_signal(
            barrier,
            inc=1,
            device_id={"wide": group_first + (group_place + d) % 4},
            device_id_type=MESH,
        )
        greeted += 1
    pl.semaphore_wait(barrier, greeted)

    sent = []

    def send(copy):
        copy.start()
        sent.append(copy)

    q_send, q_recv = q_sems
    for d in far_first(n):
        send(
            rcopy(query_ref, qfull.at[c, b, a], q_send.at[0, d], q_recv.at[0, a], dev_a((a + d) % n))
        )
    for d in range(1, 4):
        peer = group_first + (group_place + d) % 4
        send(
            rcopy(
                newkv_ref,
                kvgroup.at[group_place],
                q_send.at[3, d],
                q_recv.at[3, group_place],
                {"wide": peer},
            )
        )

    table = table_ref[...]
    place = iota((groups, blocks), 0) * blocks + iota((groups, blocks), 1) + 1
    owners = []
    for s in range(slots):
        code = jnp.max(jnp.where(table == w * slots + s, place, 0))
        live = jnp.minimum(code, 1)
        spot = jnp.maximum(code - 1, 0)
        group = spot // blocks
        slot_group[s] = group
        slot_limit[s] = live * (lengths_ref[group] - spot % blocks * BLK)
        owners.append(jnp.where(code > 0, group, -1))
    for s in range(slots):
        before = jnp.int32(slots)
        for r in range(s):
            before = jnp.where(owners[r] == owners[s], r, before)
        slot_prev[s] = before
    for g in range(groups):
        last = jnp.int32(slots)
        for s in range(slots):
            last = jnp.where(owners[s] == g, s, last)
        group_last[g] = last
    sums[slots] = jnp.zeros(sums.shape[1:], F32)

    own_query.wait()
    for d in near_first(n):
        j = (a + d) % n
        rcopy(query_ref, qfull.at[c, b, j], q_send.at[0, d], q_recv.at[0, j], dev_a(j)).wait_recv()
    for d in far_first(n):
        send(
            rcopy(
                qfull.at[c, b],
                qfull.at[c, b],
                q_send.at[1, d],
                q_recv.at[1, b],
                dev_b((b + d) % n),
            )
        )
    send(rcopy(qfull.at[c, b], qfull.at[c, b], q_send.at[2, 0], q_recv.at[2, b], sib))
    for d in near_first(n):
        j = (b + d) % n
        rcopy(
            qfull.at[c, b], qfull.at[c, j], q_send.at[1, d], q_recv.at[1, j], dev_b(j)
        ).wait_recv()
        send(rcopy(qfull.at[c, j], qfull.at[c, j], q_send.at[2, d], q_recv.at[2, j], sib))
    for j in range(n):
        rcopy(
            qfull.at[1 - c, j], qfull.at[1 - c, j], q_send.at[2, j], q_recv.at[2, j], sib
        ).wait_recv()

    loads[0].wait()
    loads[1].wait()
    half_n = n // 2
    group_rows = 4 * row_count

    def one_slot(s, carry):
        group = slot_group[s]
        gy = group // half_n
        gz = group % half_n * 2
        q = jnp.concatenate(
            [qfull[0, gy, gz], qfull[0, gy, gz + 1], qfull[1, gz, gy], qfull[1, gz + 1, gy]],
            axis=0,
        )
        q = jnp.concatenate([q[:, r * HD : (r + 1) * HD] for r in range(heads)], axis=0)
        scores = lax.dot_general(
            q, keys[s], (((1,), (1,)), ((), ())), preferred_element_type=F32
        )
        ok = iota(scores.shape, 1) < slot_limit[s]
        weights = jnp.where(ok, jnp.exp(scores * scale), 0.0).astype(BF16)
        extended = jnp.concatenate([values[s], jnp.ones((BLK, HD), BF16)], axis=1)
        sums[s] = dot(weights, extended) + sums[slot_prev[s]]
        return carry

    lax.fori_loop(0, slots, one_slot, 0)

    lane = iota((row_count, HD), 1)

    def one_group(g, carry):
        last = group_last[g]
        gy = g // half_n
        gz = g % half_n * 2
        for core in range(2):
            for zl in range(2):
                at = (core, gy, gz + zl) if core == 0 else (core, gz + zl, gy)
                dens = jnp.zeros((row_count, HD), F32)
                for r in range(heads):
                    first = r * group_rows + (core * 2 + zl) * row_count
                    block = sums[last, pl.ds(first, row_count), :]
                    part[at + (slice(None), slice(r * HD, (r + 1) * HD))] = block[:, :HD].astype(
                        BF16
                    )
                    dens = jnp.where(lane % 8 == r, block[:, HD:], dens)
                high = dens.astype(BF16).astype(F32)
                part[at + (slice(None), slice(width, width + HD))] = jnp.where(
                    lane < 8, high, dens - high
                ).astype(BF16)
        return carry

    lax.fori_loop(0, groups, one_group, 0)

    p_send, p_recv = part_sems
    for d in far_first(n) + [0]:
        j = (a + d) % n
        send(rcopy(part.at[1 - c, j], sibling_part.at[j], p_send.at[0, d], p_recv.at[0, j], sib))
    for d in far_first(n) + [0]:
        j = (b + d) % n
        rcopy(
            part.at[1 - c, j], sibling_part.at[j], p_send.at[0, d], p_recv.at[0, j], sib
        ).wait_recv()
        core_sum[j] = (part[c, j].astype(F32) + sibling_part[j].astype(F32)).astype(BF16)
        if d:
            send(rcopy(core_sum.at[j], b_parts.at[b], p_send.at[1, d], p_recv.at[1, b], dev_b(j)))

    for j in range(1, 4):
        p = (group_place + j) % 4
        rcopy(
            newkv_ref, kvgroup.at[p], q_send.at[3, j], q_recv.at[3, p], {"wide": group_first + p}
        ).wait_recv()
    own_kv.wait()
    key_rows = 4 * row_count
    tail_kv = jnp.concatenate([kvgroup[i] for i in range(4)], axis=0)
    row_id = iota((row_count, key_rows), 0)
    key_id = iota((row_count, key_rows), 1)
    wanted = jnp.full((row_count, key_rows), -1, jnp.int32)
    token_base = w // 4 * BEAMS
    for i in range(row_count // steps):
        for s in range(steps):
            beam = group_place * (row_count // steps) + i
            for j in range(s, -1, -1):
                wanted = jnp.where(
                    (row_id == i * steps + s) & (key_id % steps == j), beam, wanted
                )
                if j:
                    beam = parents_ref[token_base + beam, j - 1]
    allowed = wanted == key_id // steps
    tail_q = jnp.concatenate([query_ref[:, r * HD : (r + 1) * HD] for r in range(heads)], axis=0)
    tail_scores = lax.dot_general(
        tail_q, tail_kv[:, :HD], (((1,), (1,)), ((), ())), preferred_element_type=F32
    )
    tail_ok = jnp.concatenate([allowed.astype(F32)] * heads, axis=0)
    tail_w = jnp.where(tail_ok > 0, jnp.exp(tail_scores * scale), 0.0).astype(BF16)
    tail_num = dot(tail_w, tail_kv[:, HD:])
    tail_den = jnp.sum(tail_w.astype(F32), axis=1, keepdims=True)

    cols = n * n * MOST
    col = iota((1, cols), 1)
    col_b = col // (n * MOST)
    col_a = col // MOST % n
    col_place = col % MOST
    col_expert = col_b * n + col_a + c * ((col_a - col_b) * (n - 1))
    count = jnp.zeros((1, cols), jnp.int32)
    hits = []
    picks = []
    for r in range(row_count):
        hit = jnp.zeros((1, cols), jnp.int32)
        for i in range(top):
            hit = jnp.where(col_expert == routes_ref[r, i], 1, hit)
        picks.append(jnp.where(count == col_place, hit, 0))
        hits.append(hit)
        count = count + hit
    hit_all = jnp.concatenate(hits, axis=0)
    pick_all = jnp.concatenate(picks, axis=0).astype(F32)

    for d in near_first(n):
        j = (b + d) % n
        rcopy(core_sum.at[j], b_parts.at[j], p_send.at[1, d], p_recv.at[1, j], dev_b(j)).wait_recv()
    for d in far_first(n) + [0]:
        j = (a + d) % n
        total = core_sum[b, j].astype(F32)
        for e in range(1, n):
            total = total + b_parts[(b + e) % n, j].astype(F32)
        b_sum[j] = total.astype(BF16)
        if d:
            send(rcopy(b_sum.at[j], a_parts.at[a], p_send.at[2, d], p_recv.at[2, a], dev_a(j)))
    total = b_sum[a].astype(F32)
    for d in near_first(n):
        j = (a + d) % n
        rcopy(b_sum.at[j], a_parts.at[j], p_send.at[2, d], p_recv.at[2, j], dev_a(j)).wait_recv()
        total = total + a_parts[j].astype(F32)

    attended = []
    for r in range(heads):
        num = total[:, r * HD : (r + 1) * HD] + tail_num[r * row_count : (r + 1) * row_count]
        den = (
            total[:, width + r : width + r + 1]
            + total[:, width + 8 + r : width + 9 + r]
            + tail_den[r * row_count : (r + 1) * row_count]
        )
        attended.append((num / den).astype(BF16).astype(F32))
    residual = (stream_ref[...].astype(F32) + jnp.concatenate(attended, axis=1)).astype(BF16)
    resid[...] = residual

    x_ssem, x_rsem = x_sems
    for d in range(1, kv_count):
        send(
            rcopy(
                resid, resid_all.at[kv], x_ssem.at[0, d], x_rsem.at[0, kv], dev_x((kv + d) % kv_count)
            )
        )
    resid_all[kv] = residual
    loads[2].wait()
    for d in range(1, kv_count):
        j = (kv + d) % kv_count
        rcopy(resid, resid_all.at[j], x_ssem.at[0, d], x_rsem.at[0, j], dev_x(j)).wait_recv()
    full = jnp.concatenate([resid_all[i].astype(F32) for i in range(kv_count)], axis=1)
    mean_square = jnp.sum(full * full, axis=1, keepdims=True) / full.shape[1]
    normed = (full * lax.rsqrt(mean_square + 1e-06) * gain_ref[...]).astype(BF16)

    r_send, r_recv = row_sems
    chosen_rows = lax.dot_general(
        pick_all.astype(BF16), normed, (((0,), (0,)), ((), ())), preferred_element_type=F32
    ).astype(BF16)
    block_rows = n * MOST
    outgoing[...] = chosen_rows.reshape(outgoing.shape)
    for d in far_first(n):
        j = (b + d) % n
        send(rcopy(outgoing.at[j], mid_rows.at[b], r_send.at[0, d], r_recv.at[0, b], dev_b(j)))
    mid_rows[b] = outgoing[b]

    logits = dot(normed, router[...])
    experts = logits.shape[1]
    spread = (iota((experts, cols), 0) == col_expert).astype(F32)
    col_logits = lax.dot_general(
        logits,
        spread,
        (((1,), (0,)), ((), ())),
        preferred_element_type=F32,
        precision=lax.Precision.HIGHEST,
    )
    raised = jnp.where(hit_all > 0, jnp.exp(jnp.where(hit_all > 0, col_logits, 0.0)), 0.0)
    total_raised = jnp.sum(jnp.where(col_place == 0, raised, 0.0), axis=1, keepdims=True)
    share = raised / total_raised * pick_all
    share_high = share.astype(BF16)
    share_low = (share - share_high.astype(F32)).astype(BF16)

    out_i = iota((cols, cols), 0)
    swapped = out_i // MOST % n * block_rows + out_i // block_rows * MOST + out_i % MOST
    swap = (iota((cols, cols), 1) == swapped).astype(BF16)

    for d in near_first(n):
        j = (b + d) % n
        rcopy(outgoing.at[j], mid_rows.at[j], r_send.at[0, d], r_recv.at[0, j], dev_b(j)).wait_recv()
    model = full.shape[1]
    mid = mid_rows[...].reshape(cols, model)
    mid_perm[...] = dot(swap, mid).astype(BF16).reshape(mid_perm.shape)
    for d in far_first(n):
        j = (a + d) % n
        send(rcopy(mid_perm.at[j], rows.at[c, a], r_send.at[1, d], r_recv.at[1, a], dev_a(j)))
    send(rcopy(mid_perm.at[a], rows.at[c, a], r_send.at[2, 0], r_recv.at[2, a], sib))
    rows[c, a] = mid_perm[a]
    for d in near_first(n):
        j = (a + d) % n
        rcopy(mid_perm.at[j], rows.at[c, j], r_send.at[1, d], r_recv.at[1, j], dev_a(j)).wait_recv()
        send(rcopy(rows.at[c, j], rows.at[c, j], r_send.at[2, d], r_recv.at[2, j], sib))
    for i in range(3, 6):
        loads[i].wait()

    def expert(core):
        x = rows[core].reshape(cols, model)
        gated = dot(x, gate[...])
        lifted = dot(x, up[...])
        hidden = (gated / (1.0 + jnp.exp(-gated)) * lifted).astype(BF16)
        return dot(hidden, down[...])

    own_out = expert(c)
    for j in range(n):
        rcopy(
            rows.at[1 - c, j], rows.at[1 - c, j], r_send.at[2, j], r_recv.at[2, j], sib
        ).wait_recv()
    expert_part[...] = expert(1 - c).astype(BF16)
    e_send, e_recv = back_sems
    send(rcopy(expert_part, expert_sib, e_send.at[0, 0], e_recv.at[0, 0], sib))
    rcopy(expert_part, expert_sib, e_send.at[0, 0], e_recv.at[0, 0], sib).wait_recv()
    both = own_out + expert_sib[...].astype(F32)
    for i in range(kv_count):
        x_send[i] = both[:, i * width : (i + 1) * width].astype(BF16)
    for d in range(1, kv_count):
        j = (kv + d) % kv_count
        send(rcopy(x_send.at[j], x_recv.at[kv], e_send.at[1, d], e_recv.at[1, kv], dev_x(j)))
    mine = x_send[kv].astype(F32)
    for d in range(1, kv_count):
        j = (kv + d) % kv_count
        rcopy(x_send.at[j], x_recv.at[j], e_send.at[1, d], e_recv.at[1, j], dev_x(j)).wait_recv()
        mine = mine + x_recv[j].astype(F32)

    back_a[...] = mine.astype(BF16).reshape(back_a.shape)
    for d in far_first(n):
        j = (a + d) % n
        send(rcopy(back_a.at[j], back_mid.at[a], e_send.at[2, d], e_recv.at[2, a], dev_a(j)))
    back_mid[a] = back_a[a]
    for d in near_first(n):
        j = (a + d) % n
        rcopy(back_a.at[j], back_mid.at[j], e_send.at[2, d], e_recv.at[2, j], dev_a(j)).wait_recv()
    back_perm[...] = (
        dot(swap, back_mid[...].reshape(cols, width)).astype(BF16).reshape(back_perm.shape)
    )
    for d in far_first(n):
        j = (b + d) % n
        send(rcopy(back_perm.at[j], back_rows.at[b], e_send.at[3, d], e_recv.at[3, b], dev_b(j)))
    back_rows[b] = back_perm[b]
    for d in near_first(n):
        j = (b + d) % n
        rcopy(
            back_perm.at[j], back_rows.at[j], e_send.at[3, d], e_recv.at[3, j], dev_b(j)
        ).wait_recv()
    returned = back_rows[...].reshape(cols, width)
    combined = dot(share_high, returned) + dot(share_low, returned)
    out_ref[...] = (resid[...].astype(F32) + combined).astype(BF16)
    for copy in sent:
        copy.wait_send()


def local(
    stream_in,
    queries,
    new_kv,
    cache_keys,
    cache_values,
    lengths,
    page_table,
    parents,
    routes,
    norm_gain,
    router,
    gate_w,
    up_w,
    down_w,
):
    kv_count = lax.axis_size("kv")
    n = math.isqrt(lax.axis_size("wide") // 2)
    step_tok, steps, width = queries.shape
    rows = step_tok * steps
    heads = width // HD
    slots = cache_keys.shape[1]
    groups = lengths.shape[0]
    model = router.shape[0]
    units = gate_w.shape[2]
    cols = n * n * MOST
    block = n * MOST
    wide = width + HD
    dma = pltpu.SemaphoreType.DMA
    vmem = pltpu.VMEM
    sems = lambda stages: (dma((stages, max(n, 4))), dma((stages, max(n, 4))))
    in_vmem = pl.BlockSpec(memory_space=pltpu.VMEM)
    in_smem = pl.BlockSpec(memory_space=pltpu.SMEM)
    in_hbm = pl.BlockSpec(memory_space=pl.ANY)
    out = pl.pallas_call(
        functools.partial(kernel, n, kv_count, heads),
        out_shape=jax.ShapeDtypeStruct((rows, width), BF16),
        in_specs=[in_vmem] * 3
        + [in_hbm] * 2
        + [in_smem, in_vmem, in_smem, in_smem, in_vmem]
        + [in_hbm] * 4,
        out_specs=in_vmem,
        scratch_shapes=[
            vmem((slots, BLK, HD), BF16),
            vmem((slots, BLK, HD), BF16),
            vmem(router.shape, BF16),
            vmem((model, units), BF16),
            vmem((model, units), BF16),
            vmem((units, model), BF16),
            dma((8,)),
            vmem((2, n, n, rows, width), BF16),
            vmem((4, rows, 2 * HD), BF16),
            sems(4),
            pltpu.SMEM((slots,), jnp.int32),
            pltpu.SMEM((slots,), jnp.int32),
            pltpu.SMEM((slots,), jnp.int32),
            pltpu.SMEM((groups,), jnp.int32),
            vmem((slots + 1, 4 * rows * heads, 2 * HD), F32),
            vmem((2, n, n, rows, wide), BF16),
            vmem((n, n, rows, wide), BF16),
            vmem((n, n, rows, wide), BF16),
            vmem((n, n, rows, wide), BF16),
            vmem((n, rows, wide), BF16),
            vmem((n, rows, wide), BF16),
            sems(3),
            vmem((rows, width), BF16),
            vmem((kv_count, rows, width), BF16),
            sems(1),
            vmem((n, block, model), BF16),
            vmem((n, block, model), BF16),
            vmem((n, block, model), BF16),
            vmem((2, n, block, model), BF16),
            sems(3),
            vmem((cols, model), BF16),
            vmem((cols, model), BF16),
            vmem((kv_count, cols, width), BF16),
            vmem((kv_count, cols, width), BF16),
            vmem((n, block, width), BF16),
            vmem((n, block, width), BF16),
            vmem((n, block, width), BF16),
            vmem((n, block, width), BF16),
            sems(4),
        ],
        compiler_params=pltpu.CompilerParams(collective_id=0, has_side_effects=True),
        name="layer",
    )(
        stream_in.reshape(rows, width),
        queries.reshape(rows, width),
        new_kv.reshape(rows, 2 * HD),
        cache_keys,
        cache_values,
        lengths,
        page_table,
        parents,
        routes.reshape(rows, routes.shape[2]),
        norm_gain.reshape(1, model),
        router,
        gate_w,
        up_w,
        down_w,
    )
    return out.reshape(step_tok, steps, width)


def solution(mesh):
    return jax.shard_map(
        local,
        mesh=mesh,
        in_specs=(
            P("wide", None, "kv"),
            P("wide", None, "kv"),
            P("wide", None, None, "kv"),
            P("kv", "wide", None, None),
            P("kv", "wide", None, None),
            P(),
            P(),
            P(),
            P("wide", None, None),
            P(),
            P(),
            P("wide", None, "kv"),
            P("wide", None, "kv"),
            P("wide", "kv", None),
        ),
        out_specs=P("wide", None, "kv"),
        check_vma=False,
    )
```

```python
import functools
import math

import jax
import jax.numpy as jnp
from jax import lax
from jax.experimental import pallas as pl
from jax.experimental.pallas import tpu as pltpu
from jax.sharding import PartitionSpec as P

MESH = pl.DeviceIdType.MESH
HD = 128
BEAMS = 8
BLK = 128
MOST = 2
F32 = jnp.float32
BF16 = jnp.bfloat16


def far_first(n):
    order = sorted(range(1, n), key=lambda d: -min(d, n - d))
    return order


def near_first(n):
    return sorted(range(1, n), key=lambda d: min(d, n - d))


def rcopy(src, dst, send_sem, recv_sem, device):
    return pltpu.make_async_remote_copy(
        src_ref=src,
        dst_ref=dst,
        send_sem=send_sem,
        recv_sem=recv_sem,
        device_id=device,
        device_id_type=MESH,
    )


def dot(x, y):
    return jnp.dot(x, y, preferred_element_type=F32)


def iota(shape, axis):
    return lax.broadcasted_iota(jnp.int32, shape, axis)


def kernel(
    n,
    kv_count,
    heads,
    stream_ref,
    query_ref,
    newkv_ref,
    keys_hbm,
    values_hbm,
    lengths_ref,
    table_ref,
    parents_ref,
    routes_ref,
    gain_hbm,
    router_hbm,
    gate_hbm,
    up_hbm,
    down_hbm,
    out_ref,
    keys,
    values,
    router,
    gate,
    up,
    down,
    gain,
    load_sem,
    query,
    qfull,
    kvgroup,
    routes_b,
    q_sems,
    slot_group,
    slot_limit,
    slot_prev,
    group_last,
    sums,
    part,
    sibling_part,
    core_sum,
    b_parts,
    b_sum,
    a_parts,
    part_sems,
    resid,
    resid_all,
    x_sems,
    normed_own,
    mid_rows,
    mid_perm,
    rows,
    row_sems,
    expert_part,
    expert_sib,
    x_send,
    x_recv,
    back_a,
    back_mid,
    back_sum,
    back_rows,
    back_sems,
):
    kv = lax.axis_index("kv")
    w = lax.axis_index("wide")
    c = w % 2
    z = (w // 2) % n
    y = w // (2 * n)
    a = z + c * (y - z)
    b = y + c * (z - y)
    stride_a = 2 + c * (2 * n - 2)
    stride_b = 2 * n - c * (2 * n - 2)
    sib = {"wide": w + 1 - 2 * c}
    width = heads * HD
    row_count = query.shape[0]
    slots = keys.shape[0]
    groups = lengths_ref.shape[0]
    blocks = table_ref.shape[1]
    steps = parents_ref.shape[0] + 1
    top = routes_ref.shape[1]
    model = kv_count * width
    cols = n * n * MOST
    block_rows = n * MOST
    mids = n * row_count
    scale = 1.0 / math.sqrt(HD)

    def dev_a(j):
        return {"wide": w + (j - a) * stride_a}

    def dev_b(j):
        return {"wide": w + (j - b) * stride_b}

    def dev_x(j):
        return {"kv": j}

    group_first = w // 4 * 4
    group_place = w % 4

    loads = [
        pltpu.make_async_copy(src, dst, load_sem.at[i])
        for i, (src, dst) in enumerate(
            [
                (keys_hbm.at[0], keys),
                (values_hbm.at[0], values),
                (router_hbm, router),
                (gate_hbm.at[0], gate),
                (up_hbm.at[0], up),
                (gain_hbm, gain.at[0]),
            ]
            + [
                (down_hbm.at[0, :, i * width : (i + 1) * width], down.at[i])
                for i in range(kv_count)
            ]
        )
    ]
    for load in loads:
        load.start()
    query[...] = query_ref[...].reshape(query.shape)
    qfull[c, b, a] = query[...]
    kvgroup[group_place] = newkv_ref[...].reshape(row_count, 2 * HD)
    routes_b[b] = routes_ref[...]

    barrier = pltpu.get_barrier_semaphore()
    greeted = 0
    for d in far_first(n):
        for device in (dev_a((a + d) % n), dev_b((b + d) % n)):
            pl.semaphore_signal(barrier, inc=1, device_id=device, device_id_type=MESH)
            greeted += 1
    for d in range(1, kv_count):
        pl.semaphore_signal(
            barrier, inc=1, device_id=dev_x((kv + d) % kv_count), device_id_type=MESH
        )
        greeted += 1
    for d in range(1, 4):
        pl.semaphore_signal(
            barrier,
            inc=1,
            device_id={"wide": group_first + (group_place + d) % 4},
            device_id_type=MESH,
        )
        greeted += 1
    pl.semaphore_wait(barrier, greeted)

    sent = []

    def send(copy):
        copy.start()
        sent.append(copy)

    q_send, q_recv = q_sems
    for d in far_first(n):
        send(
            rcopy(query, qfull.at[c, b, a], q_send.at[0, d], q_recv.at[0, a], dev_a((a + d) % n))
        )
    for d in range(1, 4):
        peer = group_first + (group_place + d) % 4
        send(
            rcopy(
                kvgroup.at[group_place],
                kvgroup.at[group_place],
                q_send.at[3, d],
                q_recv.at[3, group_place],
                {"wide": peer},
            )
        )

    for d in near_first(n):
        j = (a + d) % n
        rcopy(query, qfull.at[c, b, j], q_send.at[0, d], q_recv.at[0, j], dev_a(j)).wait_recv()
    for d in far_first(n):
        send(
            rcopy(
                qfull.at[c, b],
                qfull.at[c, b],
                q_send.at[1, d],
                q_recv.at[1, b],
                dev_b((b + d) % n),
            )
        )
    send(rcopy(qfull.at[c, b], qfull.at[c, b], q_send.at[2, 0], q_recv.at[2, b], sib))
    for d in far_first(n):
        send(
            rcopy(
                routes_b.at[b],
                routes_b.at[b],
                q_send.at[4, d],
                q_recv.at[4, b],
                dev_b((b + d) % n),
            )
        )

    table = table_ref[...]
    place = iota((groups, blocks), 0) * blocks + iota((groups, blocks), 1) + 1
    owners = []
    for s in range(slots):
        code = jnp.max(jnp.where(table == w * slots + s, place, 0))
        live = jnp.minimum(code, 1)
        spot = jnp.maximum(code - 1, 0)
        group = spot // blocks
        slot_group[s] = group
        slot_limit[s] = live * (lengths_ref[group] - spot % blocks * BLK)
        owners.append(jnp.where(code > 0, group, -1))
    for s in range(slots):
        before = jnp.int32(slots)
        for r in range(s):
            before = jnp.where(owners[r] == owners[s], r, before)
        slot_prev[s] = before
    for g in range(groups):
        last = jnp.int32(slots)
        for s in range(slots):
            last = jnp.where(owners[s] == g, s, last)
        group_last[g] = last
    sums[slots] = jnp.zeros(sums.shape[1:], F32)

    for d in near_first(n):
        j = (b + d) % n
        rcopy(
            qfull.at[c, b], qfull.at[c, j], q_send.at[1, d], q_recv.at[1, j], dev_b(j)
        ).wait_recv()
        send(rcopy(qfull.at[c, j], qfull.at[c, j], q_send.at[2, d], q_recv.at[2, j], sib))
    for j in range(n):
        rcopy(
            qfull.at[1 - c, j], qfull.at[1 - c, j], q_send.at[2, j], q_recv.at[2, j], sib
        ).wait_recv()

    loads[0].wait()
    loads[1].wait()
    half_n = n // 2
    group_rows = 4 * row_count

    def one_slot(s):
        group = slot_group[s]
        gy = group // half_n
        gz = group % half_n * 2
        q = jnp.concatenate(
            [qfull[0, gy, gz], qfull[0, gy, gz + 1], qfull[1, gz, gy], qfull[1, gz + 1, gy]],
            axis=0,
        )
        q = jnp.concatenate([q[:, r * HD : (r + 1) * HD] for r in range(heads)], axis=0)
        scores = lax.dot_general(
            q, keys[s], (((1,), (1,)), ((), ())), preferred_element_type=F32
        )
        ok = iota(scores.shape, 1) < slot_limit[s]
        weights = jnp.where(ok, jnp.exp(scores * scale), 0.0).astype(BF16)
        extended = jnp.concatenate([values[s], jnp.ones((BLK, HD), BF16)], axis=1)
        sums[s] = dot(weights, extended)

    def slot_block(s, carry):
        for i in range(4):
            one_slot(s * 4 + i)
        return carry

    lax.fori_loop(0, slots // 4, slot_block, 0)

    def link_slot(s, carry):
        sums[s] = sums[s] + sums[slot_prev[s]]
        return carry

    lax.fori_loop(0, slots, link_slot, 0)

    lane = iota((row_count, HD), 1)
    tiles = n * heads
    for core in range(2):
        for j in range(n):
            part[core, j, tiles] = jnp.zeros((row_count, HD), BF16)

    def one_group(g, carry):
        last = group_last[g]
        gy = g // half_n
        gz = g % half_n * 2
        for core in range(2):
            for zl in range(2):
                bi, ai = (gy, gz + zl) if core == 0 else (gz + zl, gy)
                dens = jnp.zeros((row_count, HD), F32)
                for r in range(heads):
                    first = r * group_rows + (core * 2 + zl) * row_count
                    block = sums[last, pl.ds(first, row_count), :]
                    part[core, bi, ai * heads + r] = block[:, :HD].astype(BF16)
                    dens = jnp.where(lane % 8 == r, block[:, HD:], dens)
                old = part[core, bi, tiles].astype(F32)
                part[core, bi, tiles] = jnp.where(lane // 8 == ai, dens, old).astype(BF16)
        return carry

    lax.fori_loop(0, groups, one_group, 0)

    p_send, p_recv = part_sems
    for d in far_first(n) + [0]:
        j = (a + d) % n
        send(rcopy(part.at[1 - c, j], sibling_part.at[j], p_send.at[0, d], p_recv.at[0, j], sib))
    for d in far_first(n) + [0]:
        j = (b + d) % n
        rcopy(
            part.at[1 - c, j], sibling_part.at[j], p_send.at[0, d], p_recv.at[0, j], sib
        ).wait_recv()
        core_sum[j] = (part[c, j].astype(F32) + sibling_part[j].astype(F32)).astype(BF16)
        if d:
            send(rcopy(core_sum.at[j], b_parts.at[b], p_send.at[1, d], p_recv.at[1, b], dev_b(j)))

    for j in range(1, 4):
        p = (group_place + j) % 4
        rcopy(
            kvgroup.at[p], kvgroup.at[p], q_send.at[3, j], q_recv.at[3, p], {"wide": group_first + p}
        ).wait_recv()
    key_rows = 4 * row_count
    tail_kv = jnp.concatenate([kvgroup[i] for i in range(4)], axis=0)
    row_id = iota((row_count, key_rows), 0)
    key_id = iota((row_count, key_rows), 1)
    wanted = jnp.full((row_count, key_rows), -1, jnp.int32)
    token_base = w // 4 * BEAMS
    for i in range(row_count // steps):
        for s in range(steps):
            beam = group_place * (row_count // steps) + i
            for j in range(s, -1, -1):
                wanted = jnp.where(
                    (row_id == i * steps + s) & (key_id % steps == j), beam, wanted
                )
                if j:
                    beam = parents_ref[j - 1, token_base + beam]
    allowed = wanted == key_id // steps
    tail_q = jnp.concatenate([query[:, r * HD : (r + 1) * HD] for r in range(heads)], axis=0)
    tail_scores = lax.dot_general(
        tail_q, tail_kv[:, :HD], (((1,), (1,)), ((), ())), preferred_element_type=F32
    )
    tail_ok = jnp.concatenate([allowed.astype(F32)] * heads, axis=0)
    tail_w = jnp.where(tail_ok > 0, jnp.exp(tail_scores * scale), 0.0).astype(BF16)
    tail_num = dot(tail_w, tail_kv[:, HD:])
    tail_den = jnp.sum(tail_w.astype(F32), axis=1, keepdims=True)

    for d in near_first(n):
        j = (b + d) % n
        rcopy(
            routes_b.at[j], routes_b.at[j], q_send.at[4, d], q_recv.at[4, j], dev_b(j)
        ).wait_recv()
    routed = jnp.concatenate([routes_b[j] for j in range(n)], axis=0)
    col = iota((1, cols), 1)
    col_chip = col // block_rows
    col_source = col // MOST % n
    col_place = col % MOST
    col_expert = b * n + col_chip + c * ((col_chip - b) * (n - 1))
    experts = n * n
    source = iota((mids, 1), 0) // row_count
    expert_lane = iota((1, experts), 1)
    hit = jnp.zeros((mids, cols), F32)
    chosen = jnp.zeros((mids, experts), F32)
    for i in range(top):
        hit = jnp.where(routed[:, i : i + 1] == col_expert, 1.0, hit)
        chosen = jnp.where(routed[:, i : i + 1] == expert_lane, 1.0, chosen)
    hit = jnp.where(source == col_source, hit, 0.0)
    first_id = iota((mids, mids), 0)
    second_id = iota((mids, mids), 1)
    earlier = (first_id > second_id) & (first_id // row_count == second_id // row_count)
    taken = dot(earlier.astype(F32).astype(BF16), hit.astype(BF16))
    pick = jnp.where(taken == col_place.astype(F32), hit, 0.0)
    pick_t = jnp.transpose(pick).astype(BF16)
    spread = (iota((experts, cols), 0) == col_expert).astype(F32)

    for d in near_first(n):
        j = (b + d) % n
        rcopy(core_sum.at[j], b_parts.at[j], p_send.at[1, d], p_recv.at[1, j], dev_b(j)).wait_recv()
    dens = core_sum[b, tiles].astype(F32)
    for e in range(1, n):
        dens = dens + b_parts[(b + e) % n, tiles].astype(F32)
    dens = dens.astype(BF16)
    for d in far_first(n) + [0]:
        j = (a + d) % n
        chunk = pl.ds(j * heads, heads)
        total = core_sum[b, chunk].astype(F32)
        for e in range(1, n):
            total = total + b_parts[(b + e) % n, chunk].astype(F32)
        b_sum[j, 0:heads] = total.astype(BF16)
        b_sum[j, heads] = dens
        if d:
            send(rcopy(b_sum.at[j], a_parts.at[a], p_send.at[2, d], p_recv.at[2, a], dev_a(j)))
    total = b_sum[a].astype(F32)
    for d in near_first(n):
        j = (a + d) % n
        rcopy(b_sum.at[j], a_parts.at[j], p_send.at[2, d], p_recv.at[2, j], dev_a(j)).wait_recv()
        total = total + a_parts[j].astype(F32)

    attended = []
    for r in range(heads):
        num = total[r] + tail_num[r * row_count : (r + 1) * row_count]
        mine = jnp.sum(jnp.where(lane == a * 8 + r, total[heads], 0.0), axis=1, keepdims=True)
        den = mine + tail_den[r * row_count : (r + 1) * row_count]
        attended.append((num / den).astype(BF16).astype(F32))
    residual = (stream_ref[...].reshape(row_count, width).astype(F32) + jnp.concatenate(attended, axis=1)).astype(BF16)
    resid[...] = residual

    x_ssem, x_rsem = x_sems
    for d in range(1, kv_count):
        send(
            rcopy(
                resid, resid_all.at[kv], x_ssem.at[0, d], x_rsem.at[0, kv], dev_x((kv + d) % kv_count)
            )
        )
    resid_all[kv] = residual
    loads[2].wait()
    loads[5].wait()
    for d in range(1, kv_count):
        j = (kv + d) % kv_count
        rcopy(resid, resid_all.at[j], x_ssem.at[0, d], x_rsem.at[0, j], dev_x(j)).wait_recv()
    full = jnp.concatenate([resid_all[i].astype(F32) for i in range(kv_count)], axis=1)
    mean_square = jnp.sum(full * full, axis=1, keepdims=True) / full.shape[1]
    normed = (full * lax.rsqrt(mean_square + 1e-06) * gain[...]).astype(BF16)

    r_send, r_recv = row_sems
    normed_own[...] = normed
    for d in far_first(n):
        j = (b + d) % n
        send(rcopy(normed_own, mid_rows.at[b], r_send.at[0, d], r_recv.at[0, b], dev_b(j)))
    mid_rows[b] = normed
    for d in near_first(n):
        j = (b + d) % n
        rcopy(normed_own, mid_rows.at[j], r_send.at[0, d], r_recv.at[0, j], dev_b(j)).wait_recv()
    mid = jnp.concatenate([mid_rows[j] for j in range(n)], axis=0)
    mid_perm[...] = dot(pick_t, mid).astype(BF16).reshape(mid_perm.shape)
    for d in far_first(n):
        j = (a + d) % n
        send(rcopy(mid_perm.at[j], rows.at[c, a], r_send.at[1, d], r_recv.at[1, a], dev_a(j)))
    send(rcopy(mid_perm.at[a], rows.at[c, a], r_send.at[2, 0], r_recv.at[2, a], sib))
    rows[c, a] = mid_perm[a]

    logits = lax.dot_general(
        mid, router[...], (((1,), (1,)), ((), ())), preferred_element_type=F32
    )
    col_logits = lax.dot_general(
        logits,
        spread,
        (((1,), (0,)), ((), ())),
        preferred_element_type=F32,
        precision=lax.Precision.HIGHEST,
    )
    raised = jnp.where(chosen > 0, jnp.exp(jnp.where(chosen > 0, logits, 0.0)), 0.0)
    raised_sum = jnp.sum(raised, axis=1, keepdims=True)
    share = jnp.where(pick > 0, jnp.exp(jnp.where(pick > 0, col_logits, 0.0)), 0.0) / raised_sum
    share_high = share.astype(BF16)
    share_low = (share - share_high.astype(F32)).astype(BF16)

    for d in near_first(n):
        j = (a + d) % n
        rcopy(mid_perm.at[j], rows.at[c, j], r_send.at[1, d], r_recv.at[1, j], dev_a(j)).wait_recv()
        send(rcopy(rows.at[c, j], rows.at[c, j], r_send.at[2, d], r_recv.at[2, j], sib))
    loads[3].wait()
    loads[4].wait()

    def hidden(core):
        x = rows[core].reshape(cols, model)
        gated = lax.dot_general(
            x, gate[...], (((1,), (1,)), ((), ())), preferred_element_type=F32
        )
        lifted = lax.dot_general(
            x, up[...], (((1,), (1,)), ((), ())), preferred_element_type=F32
        )
        return (gated / (1.0 + jnp.exp(-gated)) * lifted).astype(BF16)

    own_hidden = hidden(c)
    for j in range(n):
        rcopy(
            rows.at[1 - c, j], rows.at[1 - c, j], r_send.at[2, j], r_recv.at[2, j], sib
        ).wait_recv()
    sib_hidden = hidden(1 - c)
    for load in loads[6:]:
        load.wait()
    e_send, e_recv = back_sems
    slices = far_first(kv_count) + [0]
    for d in slices:
        i = (kv + d) % kv_count
        expert_part[i] = dot(sib_hidden, down[i]).astype(BF16)
        send(rcopy(expert_part.at[i], expert_sib.at[i], e_send.at[0, d], e_recv.at[0, i], sib))
    for d in slices:
        i = (kv + d) % kv_count
        own_out = dot(own_hidden, down[i])
        rcopy(
            expert_part.at[i], expert_sib.at[i], e_send.at[0, d], e_recv.at[0, i], sib
        ).wait_recv()
        both = own_out + expert_sib[i].astype(F32)
        if d:
            x_send[i] = both.astype(BF16)
            send(rcopy(x_send.at[i], x_recv.at[kv], e_send.at[1, d], e_recv.at[1, kv], dev_x(i)))
    mine = both
    for d in range(1, kv_count):
        j = (kv + d) % kv_count
        rcopy(x_send.at[j], x_recv.at[j], e_send.at[1, d], e_recv.at[1, j], dev_x(j)).wait_recv()
        mine = mine + x_recv[j].astype(F32)

    back_a[...] = mine.astype(BF16).reshape(back_a.shape)
    for d in far_first(n):
        j = (a + d) % n
        send(rcopy(back_a.at[j], back_mid.at[a], e_send.at[2, d], e_recv.at[2, a], dev_a(j)))
    back_mid[a] = back_a[a]
    for d in near_first(n):
        j = (a + d) % n
        rcopy(back_a.at[j], back_mid.at[j], e_send.at[2, d], e_recv.at[2, j], dev_a(j)).wait_recv()
    returned = back_mid[...].reshape(cols, width)
    weighted = dot(share_high, returned) + dot(share_low, returned)
    back_sum[...] = weighted.astype(BF16).reshape(back_sum.shape)
    for d in far_first(n):
        j = (b + d) % n
        send(rcopy(back_sum.at[j], back_rows.at[b], e_send.at[3, d], e_recv.at[3, b], dev_b(j)))
    combined = resid[...].astype(F32) + back_sum[b].astype(F32)
    for d in near_first(n):
        j = (b + d) % n
        rcopy(
            back_sum.at[j], back_rows.at[j], e_send.at[3, d], e_recv.at[3, j], dev_b(j)
        ).wait_recv()
        combined = combined + back_rows[j].astype(F32)
    out_ref[...] = combined.astype(BF16).reshape(out_ref.shape)
    for copy in sent:
        copy.wait_send()


def local(
    stream_in,
    queries,
    new_kv,
    cache_keys,
    cache_values,
    lengths,
    page_table,
    parents,
    routes,
    norm_gain,
    router,
    gate_w,
    up_w,
    down_w,
):
    kv_count = lax.axis_size("kv")
    n = math.isqrt(lax.axis_size("wide") // 2)
    step_tok, steps, width = queries.shape
    rows = step_tok * steps
    heads = width // HD
    slots = cache_keys.shape[1]
    groups = lengths.shape[0]
    model = router.shape[0]
    units = gate_w.shape[2]
    cols = n * n * MOST
    block = n * MOST
    tiles = n * heads + 1
    dma = pltpu.SemaphoreType.DMA
    vmem = pltpu.VMEM
    sems = lambda stages: (dma((stages, max(n, 4))), dma((stages, max(n, 4))))
    in_vmem = pl.BlockSpec(memory_space=pltpu.VMEM)
    in_smem = pl.BlockSpec(memory_space=pltpu.SMEM)
    in_hbm = pl.BlockSpec(memory_space=pl.ANY)
    return pl.pallas_call(
        functools.partial(kernel, n, kv_count, heads),
        out_shape=jax.ShapeDtypeStruct(stream_in.shape, BF16),
        in_specs=[in_vmem] * 3
        + [in_hbm] * 2
        + [in_smem, in_vmem, in_smem, in_vmem]
        + [in_hbm] * 5,
        out_specs=in_vmem,
        scratch_shapes=[
            vmem((slots, BLK, HD), BF16),
            vmem((slots, BLK, HD), BF16),
            vmem((router.shape[1], model), BF16),
            vmem((units, model), BF16),
            vmem((units, model), BF16),
            vmem((kv_count, units, width), BF16),
            vmem((1, model), F32),
            dma((6 + kv_count,)),
            vmem((rows, width), BF16),
            vmem((2, n, n, rows, width), BF16),
            vmem((4, rows, 2 * HD), BF16),
            vmem((n, rows, routes.shape[2]), jnp.int32),
            sems(5),
            pltpu.SMEM((slots,), jnp.int32),
            pltpu.SMEM((slots,), jnp.int32),
            pltpu.SMEM((slots,), jnp.int32),
            pltpu.SMEM((groups,), jnp.int32),
            vmem((slots + 1, 4 * rows * heads, 2 * HD), F32),
            vmem((2, n, tiles, rows, HD), BF16),
            vmem((n, tiles, rows, HD), BF16),
            vmem((n, tiles, rows, HD), BF16),
            vmem((n, tiles, rows, HD), BF16),
            vmem((n, heads + 1, rows, HD), BF16),
            vmem((n, heads + 1, rows, HD), BF16),
            sems(3),
            vmem((rows, width), BF16),
            vmem((kv_count, rows, width), BF16),
            sems(1),
            vmem((rows, model), BF16),
            vmem((n, rows, model), BF16),
            vmem((n, block, model), BF16),
            vmem((2, n, block, model), BF16),
            sems(3),
            vmem((kv_count, cols, width), BF16),
            vmem((kv_count, cols, width), BF16),
            vmem((kv_count, cols, width), BF16),
            vmem((kv_count, cols, width), BF16),
            vmem((n, block, width), BF16),
            vmem((n, block, width), BF16),
            vmem((n, rows, width), BF16),
            vmem((n, rows, width), BF16),
            sems(4),
        ],
        compiler_params=pltpu.CompilerParams(collective_id=0, has_side_effects=True),
        name="layer",
    )(
        stream_in,
        queries,
        new_kv,
        cache_keys,
        cache_values,
        lengths,
        page_table,
        jnp.swapaxes(parents, 0, 1),
        routes.reshape(rows, routes.shape[2]),
        norm_gain,
        jnp.swapaxes(router, 0, 1),
        jnp.swapaxes(gate_w, 1, 2),
        jnp.swapaxes(up_w, 1, 2),
        down_w,
    )


def solution(mesh):
    return jax.shard_map(
        local,
        mesh=mesh,
        in_specs=(
            P("wide", None, "kv"),
            P("wide", None, "kv"),
            P("wide", None, None, "kv"),
            P("kv", "wide", None, None),
            P("kv", "wide", None, None),
            P(),
            P(),
            P(),
            P("wide", None, None),
            P(),
            P(),
            P("wide", None, "kv"),
            P("wide", None, "kv"),
            P("wide", "kv", None),
        ),
        out_specs=P("wide", None, "kv"),
        check_vma=False,
    )
```

```python
import functools
import math

import jax
import jax.numpy as jnp
from jax import lax
from jax.experimental import pallas as pl
from jax.experimental.pallas import tpu as pltpu
from jax.sharding import PartitionSpec as P

MESH = pl.DeviceIdType.MESH
HD = 128
BEAMS = 8
BLK = 128
MOST = 2
F32 = jnp.float32
BF16 = jnp.bfloat16


def far_first(n):
    order = sorted(range(1, n), key=lambda d: -min(d, n - d))
    return order


def near_first(n):
    return sorted(range(1, n), key=lambda d: min(d, n - d))


def rcopy(src, dst, send_sem, recv_sem, device):
    return pltpu.make_async_remote_copy(
        src_ref=src,
        dst_ref=dst,
        send_sem=send_sem,
        recv_sem=recv_sem,
        device_id=device,
        device_id_type=MESH,
    )


def dot(x, y):
    return jnp.dot(x, y, preferred_element_type=F32)


def iota(shape, axis):
    return lax.broadcasted_iota(jnp.int32, shape, axis)


def kernel(
    n,
    kv_count,
    heads,
    stream_ref,
    query_ref,
    newkv_ref,
    keys_hbm,
    values_hbm,
    lengths_ref,
    table_ref,
    parents_ref,
    routes_ref,
    gain_hbm,
    router_hbm,
    gate_hbm,
    up_hbm,
    down_hbm,
    out_ref,
    keys,
    values,
    router,
    gate,
    up,
    down,
    gain,
    load_sem,
    query,
    query_parts,
    q_all,
    kvgroup,
    routes_b,
    q_sems,
    slot_group,
    slot_limit,
    slot_prev,
    group_last,
    sums_all,
    part_all,
    sibling_part,
    core_sum_all,
    b_parts,
    b_sum,
    a_parts,
    part_sems,
    resid,
    mid_resid,
    x_sems,
    mid_perm,
    rows,
    row_sems,
    expert_part,
    expert_sib,
    x_send,
    back_mid,
    back_sum,
    back_rows,
    back_sems,
):
    kv = lax.axis_index("kv")
    w = lax.axis_index("wide")
    c = w % 2
    z = (w // 2) % n
    y = w // (2 * n)
    a = z + c * (y - z)
    b = y + c * (z - y)
    stride_a = 2 + c * (2 * n - 2)
    stride_b = 2 * n - c * (2 * n - 2)
    sib = {"wide": w + 1 - 2 * c}
    width = heads * HD
    row_count = query.shape[0]
    slots = keys.shape[0]
    groups = lengths_ref.shape[0]
    blocks = table_ref.shape[1]
    steps = parents_ref.shape[0] + 1
    top = routes_ref.shape[1]
    model = kv_count * width
    cols = n * n * MOST
    block_rows = n * MOST
    mids = n * row_count
    scale = 1.0 / math.sqrt(HD)

    def dev_a(j):
        return {"wide": w + (j - a) * stride_a}

    def dev_b(j):
        return {"wide": w + (j - b) * stride_b}

    def dev_xa(i, j):
        return {"kv": i, "wide": w + (j - a) * stride_a}

    def dev_xb(i, j):
        return {"kv": i, "wide": w + (j - b) * stride_b}

    spans = [(0, (heads + 1) // 2), ((heads + 1) // 2, heads)]

    group_first = w // 4 * 4
    group_place = w % 4

    loads = [
        pltpu.make_async_copy(src, dst, load_sem.at[i])
        for i, (src, dst) in enumerate(
            [
                (keys_hbm.at[0], keys),
                (values_hbm.at[0], values),
                (router_hbm, router),
                (gate_hbm.at[0], gate),
                (up_hbm.at[0], up),
                (gain_hbm, gain.at[0]),
            ]
            + [
                (down_hbm.at[0, :, i * width : (i + 1) * width], down.at[i])
                for i in range(kv_count)
            ]
        )
    ]
    for load in loads:
        load.start()
    query[...] = query_ref[...].reshape(query.shape)
    for (first, last), share_q, all_q in zip(spans, query_parts, q_all):
        share_q[...] = query[:, first * HD : last * HD]
        all_q[c, b, a] = share_q[...]
    kvgroup[group_place] = newkv_ref[...].reshape(row_count, 2 * HD)
    routes_b[b] = routes_ref[...]

    barrier = pltpu.get_barrier_semaphore()
    greeted = 0
    line = far_first(n)
    for dx in range(kv_count):
        i = (kv + dx) % kv_count
        devices = [dev_xa(i, (a + d) % n) for d in line] + [dev_xb(i, (b + d) % n) for d in line]
        if dx:
            devices.append(dev_xa(i, a))
        for device in devices:
            pl.semaphore_signal(barrier, inc=1, device_id=device, device_id_type=MESH)
            greeted += 1
    for d in range(1, 4):
        pl.semaphore_signal(
            barrier,
            inc=1,
            device_id={"wide": group_first + (group_place + d) % 4},
            device_id_type=MESH,
        )
        greeted += 1
    pl.semaphore_wait(barrier, greeted)

    sent = []

    def send(copy):
        copy.start()
        sent.append(copy)

    q_send, q_recv = q_sems
    for ch, share_q in enumerate(query_parts):
        for d in far_first(n):
            send(
                rcopy(
                    share_q,
                    q_all[ch].at[c, b, a],
                    q_send.at[7 * ch, d],
                    q_recv.at[7 * ch, a],
                    dev_a((a + d) % n),
                )
            )
    for d in range(1, 4):
        peer = group_first + (group_place + d) % 4
        send(
            rcopy(
                kvgroup.at[group_place],
                kvgroup.at[group_place],
                q_send.at[3, d],
                q_recv.at[3, group_place],
                {"wide": peer},
            )
        )

    for ch in range(2):
        for d in near_first(n):
            j = (a + d) % n
            rcopy(
                query_parts[ch], q_all[ch].at[c, b, j], q_send.at[7 * ch, d], q_recv.at[7 * ch, j], dev_a(j)
            ).wait_recv()
        block = q_all[ch].at[c, b]
        for d in far_first(n):
            send(
                rcopy(
                    block, block, q_send.at[1 + 4 * ch, d], q_recv.at[1 + 4 * ch, b], dev_b((b + d) % n)
                )
            )
        send(rcopy(block, block, q_send.at[2 + 4 * ch, 0], q_recv.at[2 + 4 * ch, b], sib))
    for d in far_first(n):
        send(
            rcopy(
                routes_b.at[b],
                routes_b.at[b],
                q_send.at[4, d],
                q_recv.at[4, b],
                dev_b((b + d) % n),
            )
        )

    table = table_ref[...]
    place = iota((groups, blocks), 0) * blocks + iota((groups, blocks), 1) + 1
    owners = []
    for s in range(slots):
        code = jnp.max(jnp.where(table == w * slots + s, place, 0))
        live = jnp.minimum(code, 1)
        spot = jnp.maximum(code - 1, 0)
        group = spot // blocks
        slot_group[s] = group
        slot_limit[s] = live * (lengths_ref[group] - spot % blocks * BLK)
        owners.append(jnp.where(code > 0, group, -1))
    for s in range(slots):
        before = jnp.int32(slots)
        for r in range(s):
            before = jnp.where(owners[r] == owners[s], r, before)
        slot_prev[s] = before
    for g in range(groups):
        last = jnp.int32(slots)
        for s in range(slots):
            last = jnp.where(owners[s] == g, s, last)
        group_last[g] = last

    def pass_on(ch):
        for d in near_first(n):
            j = (b + d) % n
            block = q_all[ch].at[c, j]
            rcopy(
                block, block, q_send.at[1 + 4 * ch, d], q_recv.at[1 + 4 * ch, j], dev_b(j)
            ).wait_recv()
            send(rcopy(block, block, q_send.at[2 + 4 * ch, d], q_recv.at[2 + 4 * ch, j], sib))

    def await_sibling(ch):
        for j in range(n):
            block = q_all[ch].at[1 - c, j]
            rcopy(
                block, block, q_send.at[2 + 4 * ch, j], q_recv.at[2 + 4 * ch, j], sib
            ).wait_recv()

    half_n = n // 2
    group_rows = 4 * row_count
    lane = iota((row_count, HD), 1)
    p_send, p_recv = part_sems

    def attend(ch):
        first_head, last_head = spans[ch]
        count = last_head - first_head
        sums, part = sums_all[ch], part_all[ch]
        tiles = n * count
        qfull = q_all[ch]

        def one_slot(s):
            group = slot_group[s]
            gy = group // half_n
            gz = group % half_n * 2
            q = jnp.concatenate(
                [
                    qfull[0, gy, gz],
                    qfull[0, gy, gz + 1],
                    qfull[1, gz, gy],
                    qfull[1, gz + 1, gy],
                ],
                axis=0,
            )
            q = jnp.concatenate([q[:, r * HD : (r + 1) * HD] for r in range(count)], axis=0)
            scores = lax.dot_general(
                q, keys[s], (((1,), (1,)), ((), ())), preferred_element_type=F32
            )
            ok = iota(scores.shape, 1) < slot_limit[s]
            weights = jnp.where(ok, jnp.exp(scores * scale), 0.0).astype(BF16)
            extended = jnp.concatenate([values[s], jnp.ones((BLK, HD), BF16)], axis=1)
            sums[s] = dot(weights, extended)

        def slot_block(s, carry):
            for i in range(4):
                one_slot(s * 4 + i)
            return carry

        sums[slots] = jnp.zeros(sums.shape[1:], F32)
        lax.fori_loop(0, slots // 4, slot_block, 0)

        def link_slot(s, carry):
            sums[s] = sums[s] + sums[slot_prev[s]]
            return carry

        lax.fori_loop(0, slots, link_slot, 0)

        for core in range(2):
            for j in range(n):
                part[core, j, tiles] = jnp.zeros((row_count, HD), BF16)

        def one_group(g, carry):
            last = group_last[g]
            gy = g // half_n
            gz = g % half_n * 2
            for core in range(2):
                for zl in range(2):
                    bi, ai = (gy, gz + zl) if core == 0 else (gz + zl, gy)
                    dens = jnp.zeros((row_count, HD), F32)
                    for r in range(count):
                        first = r * group_rows + (core * 2 + zl) * row_count
                        block = sums[last, pl.ds(first, row_count), :]
                        part[core, bi, ai * count + r] = block[:, :HD].astype(BF16)
                        dens = jnp.where(lane % 8 == r, block[:, HD:], dens)
                    old = part[core, bi, tiles].astype(F32)
                    part[core, bi, tiles] = jnp.where(lane // 8 == ai, dens, old).astype(BF16)
            return carry

        lax.fori_loop(0, groups, one_group, 0)
        for d in far_first(n) + [0]:
            j = (a + d) % n
            send(
                rcopy(
                    part.at[1 - c, j],
                    sibling_part[ch].at[j],
                    p_send.at[3 * ch, d],
                    p_recv.at[3 * ch, j],
                    sib,
                )
            )

    def sum_cores(ch):
        part, core_sum = part_all[ch], core_sum_all[ch]
        for d in far_first(n) + [0]:
            j = (b + d) % n
            rcopy(
                part.at[1 - c, j],
                sibling_part[ch].at[j],
                p_send.at[3 * ch, d],
                p_recv.at[3 * ch, j],
                sib,
            ).wait_recv()
            core_sum[j] = (part[c, j].astype(F32) + sibling_part[ch][j].astype(F32)).astype(BF16)
            if d:
                send(
                    rcopy(
                        core_sum.at[j],
                        b_parts[ch].at[b],
                        p_send.at[3 * ch + 1, d],
                        p_recv.at[3 * ch + 1, b],
                        dev_b(j),
                    )
                )

    pass_on(0)
    await_sibling(0)
    loads[0].wait()
    loads[1].wait()
    attend(0)
    pass_on(1)
    sum_cores(0)
    await_sibling(1)
    attend(1)
    sum_cores(1)

    for j in range(1, 4):
        p = (group_place + j) % 4
        rcopy(
            kvgroup.at[p], kvgroup.at[p], q_send.at[3, j], q_recv.at[3, p], {"wide": group_first + p}
        ).wait_recv()
    key_rows = 4 * row_count
    tail_kv = jnp.concatenate([kvgroup[i] for i in range(4)], axis=0)
    row_id = iota((row_count, key_rows), 0)
    key_id = iota((row_count, key_rows), 1)
    wanted = jnp.full((row_count, key_rows), -1, jnp.int32)
    token_base = w // 4 * BEAMS
    for i in range(row_count // steps):
        for s in range(steps):
            beam = group_place * (row_count // steps) + i
            for j in range(s, -1, -1):
                wanted = jnp.where(
                    (row_id == i * steps + s) & (key_id % steps == j), beam, wanted
                )
                if j:
                    beam = parents_ref[j - 1, token_base + beam]
    allowed = wanted == key_id // steps
    tail_q = jnp.concatenate([query[:, r * HD : (r + 1) * HD] for r in range(heads)], axis=0)
    tail_scores = lax.dot_general(
        tail_q, tail_kv[:, :HD], (((1,), (1,)), ((), ())), preferred_element_type=F32
    )
    tail_ok = jnp.concatenate([allowed.astype(F32)] * heads, axis=0)
    tail_w = jnp.where(tail_ok > 0, jnp.exp(tail_scores * scale), 0.0).astype(BF16)
    tail_num = dot(tail_w, tail_kv[:, HD:])
    tail_den = jnp.sum(tail_w.astype(F32), axis=1, keepdims=True)

    for d in near_first(n):
        j = (b + d) % n
        rcopy(
            routes_b.at[j], routes_b.at[j], q_send.at[4, d], q_recv.at[4, j], dev_b(j)
        ).wait_recv()
    routed = jnp.concatenate([routes_b[j] for j in range(n)], axis=0)
    col = iota((1, cols), 1)
    col_chip = col // block_rows
    col_source = col // MOST % n
    col_place = col % MOST
    col_expert = b * n + col_chip + c * ((col_chip - b) * (n - 1))
    experts = n * n
    source = iota((mids, 1), 0) // row_count
    expert_lane = iota((1, experts), 1)
    hit = jnp.zeros((mids, cols), F32)
    chosen = jnp.zeros((mids, experts), F32)
    for i in range(top):
        hit = jnp.where(routed[:, i : i + 1] == col_expert, 1.0, hit)
        chosen = jnp.where(routed[:, i : i + 1] == expert_lane, 1.0, chosen)
    hit = jnp.where(source == col_source, hit, 0.0)
    first_id = iota((mids, mids), 0)
    second_id = iota((mids, mids), 1)
    earlier = (first_id > second_id) & (first_id // row_count == second_id // row_count)
    taken = dot(earlier.astype(F32).astype(BF16), hit.astype(BF16))
    pick = jnp.where(taken == col_place.astype(F32), hit, 0.0)
    pick_t = jnp.transpose(pick).astype(BF16)
    spread = (iota((experts, cols), 0) == col_expert).astype(F32)

    for ch, (first_head, last_head) in enumerate(spans):
        count = last_head - first_head
        core_sum, part_b, sum_b = core_sum_all[ch], b_parts[ch], b_sum[ch]
        for d in near_first(n):
            j = (b + d) % n
            rcopy(
                core_sum.at[j], part_b.at[j], p_send.at[3 * ch + 1, d], p_recv.at[3 * ch + 1, j], dev_b(j)
            ).wait_recv()
        dens = core_sum[b, n * count].astype(F32)
        for e in range(1, n):
            dens = dens + part_b[(b + e) % n, n * count].astype(F32)
        dens = dens.astype(BF16)
        for d in far_first(n) + [0]:
            j = (a + d) % n
            chunk = pl.ds(j * count, count)
            total = core_sum[b, chunk].astype(F32)
            for e in range(1, n):
                total = total + part_b[(b + e) % n, chunk].astype(F32)
            sum_b[j, 0:count] = total.astype(BF16)
            sum_b[j, count] = dens
            if d:
                send(
                    rcopy(
                        sum_b.at[j],
                        a_parts[ch].at[a],
                        p_send.at[3 * ch + 2, d],
                        p_recv.at[3 * ch + 2, a],
                        dev_a(j),
                    )
                )
    nums = []
    dens = []
    for ch, (first_head, last_head) in enumerate(spans):
        count = last_head - first_head
        total = b_sum[ch][a].astype(F32)
        for d in near_first(n):
            j = (a + d) % n
            rcopy(
                b_sum[ch].at[j], a_parts[ch].at[j], p_send.at[3 * ch + 2, d], p_recv.at[3 * ch + 2, j], dev_a(j)
            ).wait_recv()
            total = total + a_parts[ch][j].astype(F32)
        for r in range(count):
            nums.append(total[r])
            mine = jnp.where(lane == a * 8 + r, total[count], 0.0)
            dens.append(jnp.sum(mine, axis=1, keepdims=True))

    attended = []
    for r in range(heads):
        num = nums[r] + tail_num[r * row_count : (r + 1) * row_count]
        den = dens[r] + tail_den[r * row_count : (r + 1) * row_count]
        attended.append((num / den).astype(BF16).astype(F32))
    residual = (stream_ref[...].reshape(row_count, width).astype(F32) + jnp.concatenate(attended, axis=1)).astype(BF16)
    resid[...] = residual

    x_ssem, x_rsem = x_sems
    spots = [(dx, d) for d in far_first(n) + [0] for dx in far_first(kv_count) + [0]]
    for dx, d in spots[:-1]:
        device = dev_xb((kv + dx) % kv_count, (b + d) % n)
        send(
            rcopy(
                resid,
                mid_resid.at[b, kv],
                x_ssem.at[0, dx * n + d],
                x_rsem.at[0, kv * n + b],
                device,
            )
        )
    mid_resid[b, kv] = residual
    loads[2].wait()
    loads[5].wait()
    for dx, d in reversed(spots[:-1]):
        i, j = (kv + dx) % kv_count, (b + d) % n
        rcopy(
            resid, mid_resid.at[j, i], x_ssem.at[0, dx * n + d], x_rsem.at[0, i * n + j], dev_xb(i, j)
        ).wait_recv()
    full = jnp.concatenate(
        [
            jnp.concatenate([mid_resid[j, i] for j in range(n)], axis=0).astype(F32)
            for i in range(kv_count)
        ],
        axis=1,
    )
    mean_square = jnp.sum(full * full, axis=1, keepdims=True) / model
    mid = (full * lax.rsqrt(mean_square + 1e-06) * gain[...]).astype(BF16)

    r_send, r_recv = row_sems
    mid_perm[...] = dot(pick_t, mid).astype(BF16).reshape(mid_perm.shape)
    for d in far_first(n):
        j = (a + d) % n
        send(rcopy(mid_perm.at[j], rows.at[c, a], r_send.at[1, d], r_recv.at[1, a], dev_a(j)))
    send(rcopy(mid_perm.at[a], rows.at[c, a], r_send.at[2, 0], r_recv.at[2, a], sib))
    rows[c, a] = mid_perm[a]

    logits = lax.dot_general(
        mid, router[...], (((1,), (1,)), ((), ())), preferred_element_type=F32
    )
    col_logits = lax.dot_general(
        logits,
        spread,
        (((1,), (0,)), ((), ())),
        preferred_element_type=F32,
        precision=lax.Precision.HIGHEST,
    )
    raised = jnp.where(chosen > 0, jnp.exp(jnp.where(chosen > 0, logits, 0.0)), 0.0)
    raised_sum = jnp.sum(raised, axis=1, keepdims=True)
    share = jnp.where(pick > 0, jnp.exp(jnp.where(pick > 0, col_logits, 0.0)), 0.0) / raised_sum
    share_high = share.astype(BF16)
    share_low = (share - share_high.astype(F32)).astype(BF16)

    for d in near_first(n):
        j = (a + d) % n
        rcopy(mid_perm.at[j], rows.at[c, j], r_send.at[1, d], r_recv.at[1, j], dev_a(j)).wait_recv()
        send(rcopy(rows.at[c, j], rows.at[c, j], r_send.at[2, d], r_recv.at[2, j], sib))
    loads[3].wait()
    loads[4].wait()

    def hidden(core):
        x = rows[core].reshape(cols, model)
        gated = lax.dot_general(
            x, gate[...], (((1,), (1,)), ((), ())), preferred_element_type=F32
        )
        lifted = lax.dot_general(
            x, up[...], (((1,), (1,)), ((), ())), preferred_element_type=F32
        )
        return (gated / (1.0 + jnp.exp(-gated)) * lifted).astype(BF16)

    own_hidden = hidden(c)
    for j in range(n):
        rcopy(
            rows.at[1 - c, j], rows.at[1 - c, j], r_send.at[2, j], r_recv.at[2, j], sib
        ).wait_recv()
    sib_hidden = hidden(1 - c)
    for load in loads[6:]:
        load.wait()
    e_send, e_recv = back_sems
    slices = far_first(kv_count) + [0]
    for d in slices:
        i = (kv + d) % kv_count
        expert_part[i] = dot(sib_hidden, down[i]).astype(BF16)
        send(rcopy(expert_part.at[i], expert_sib.at[i], e_send.at[0, d], e_recv.at[0, i], sib))
    for d in slices:
        i = (kv + d) % kv_count
        own_out = dot(own_hidden, down[i])
        rcopy(
            expert_part.at[i], expert_sib.at[i], e_send.at[0, d], e_recv.at[0, i], sib
        ).wait_recv()
        both = own_out + expert_sib[i].astype(F32)
        x_send[i] = both.astype(BF16).reshape(x_send.shape[1:])
        for da in far_first(n) + [0]:
            j = (a + da) % n
            if d or da:
                send(
                    rcopy(
                        x_send.at[i, j],
                        back_mid.at[kv, a],
                        x_ssem.at[1, d * n + da],
                        x_rsem.at[1, kv * n + a],
                        dev_xa(i, j),
                    )
                )
    back_mid[kv, a] = x_send[kv, a]

    shares = [jnp.concatenate([part] * kv_count, axis=1) for part in (share_high, share_low)]
    for dx, d in [(dx, d) for d in [0] + near_first(n) for dx in range(kv_count)][1:]:
        i, j = (kv + dx) % kv_count, (a + d) % n
        rcopy(
            x_send.at[i, j], back_mid.at[i, j], x_ssem.at[1, dx * n + d], x_rsem.at[1, i * n + j], dev_xa(i, j)
        ).wait_recv()
    returned = back_mid[...].reshape(kv_count * cols, width)
    weighted = dot(shares[0], returned) + dot(shares[1], returned)
    back_sum[...] = weighted.astype(BF16).reshape(back_sum.shape)
    for d in far_first(n):
        j = (b + d) % n
        send(rcopy(back_sum.at[j], back_rows.at[b], e_send.at[3, d], e_recv.at[3, b], dev_b(j)))
    combined = resid[...].astype(F32) + back_sum[b].astype(F32)
    for d in near_first(n):
        j = (b + d) % n
        rcopy(
            back_sum.at[j], back_rows.at[j], e_send.at[3, d], e_recv.at[3, j], dev_b(j)
        ).wait_recv()
        combined = combined + back_rows[j].astype(F32)
    out_ref[...] = combined.astype(BF16).reshape(out_ref.shape)
    for copy in sent:
        copy.wait_send()


def local(
    stream_in,
    queries,
    new_kv,
    cache_keys,
    cache_values,
    lengths,
    page_table,
    parents,
    routes,
    norm_gain,
    router,
    gate_w,
    up_w,
    down_w,
):
    kv_count = lax.axis_size("kv")
    n = math.isqrt(lax.axis_size("wide") // 2)
    step_tok, steps, width = queries.shape
    rows = step_tok * steps
    heads = width // HD
    slots = cache_keys.shape[1]
    groups = lengths.shape[0]
    model = router.shape[0]
    units = gate_w.shape[2]
    cols = n * n * MOST
    block = n * MOST
    spans = [(heads + 1) // 2, heads // 2]
    per_span = lambda shape, dtype: [vmem(shape(count), dtype) for count in spans]
    dma = pltpu.SemaphoreType.DMA
    vmem = pltpu.VMEM
    sems = lambda stages: (dma((stages, max(n, 4))), dma((stages, max(n, 4))))
    in_vmem = pl.BlockSpec(memory_space=pltpu.VMEM)
    in_smem = pl.BlockSpec(memory_space=pltpu.SMEM)
    in_hbm = pl.BlockSpec(memory_space=pl.ANY)
    return pl.pallas_call(
        functools.partial(kernel, n, kv_count, heads),
        out_shape=jax.ShapeDtypeStruct(stream_in.shape, BF16),
        in_specs=[in_vmem] * 3
        + [in_hbm] * 2
        + [in_smem, in_vmem, in_smem, in_vmem]
        + [in_hbm] * 5,
        out_specs=in_vmem,
        scratch_shapes=[
            vmem((slots, BLK, HD), BF16),
            vmem((slots, BLK, HD), BF16),
            vmem((router.shape[1], model), BF16),
            vmem((units, model), BF16),
            vmem((units, model), BF16),
            vmem((kv_count, units, width), BF16),
            vmem((1, model), F32),
            dma((6 + kv_count,)),
            vmem((rows, width), BF16),
            per_span(lambda k: (rows, k * HD), BF16),
            per_span(lambda k: (2, n, n, rows, k * HD), BF16),
            vmem((4, rows, 2 * HD), BF16),
            vmem((n, rows, routes.shape[2]), jnp.int32),
            sems(8),
            pltpu.SMEM((slots,), jnp.int32),
            pltpu.SMEM((slots,), jnp.int32),
            pltpu.SMEM((slots,), jnp.int32),
            pltpu.SMEM((groups,), jnp.int32),
            per_span(lambda k: (slots + 1, 4 * rows * k, 2 * HD), F32),
            per_span(lambda k: (2, n, n * k + 1, rows, HD), BF16),
            per_span(lambda k: (n, n * k + 1, rows, HD), BF16),
            per_span(lambda k: (n, n * k + 1, rows, HD), BF16),
            per_span(lambda k: (n, n * k + 1, rows, HD), BF16),
            per_span(lambda k: (n, k + 1, rows, HD), BF16),
            per_span(lambda k: (n, k + 1, rows, HD), BF16),
            sems(6),
            vmem((rows, width), BF16),
            vmem((n, kv_count, rows, width), BF16),
            (dma((2, kv_count * n)), dma((2, kv_count * n))),
            vmem((n, block, model), BF16),
            vmem((2, n, block, model), BF16),
            sems(3),
            vmem((kv_count, cols, width), BF16),
            vmem((kv_count, cols, width), BF16),
            vmem((kv_count, n, block, width), BF16),
            vmem((kv_count, n, block, width), BF16),
            vmem((n, rows, width), BF16),
            vmem((n, rows, width), BF16),
            sems(4),
        ],
        compiler_params=pltpu.CompilerParams(collective_id=0, has_side_effects=True),
        name="layer",
    )(
        stream_in,
        queries,
        new_kv,
        cache_keys,
        cache_values,
        lengths,
        page_table,
        jnp.swapaxes(parents, 0, 1),
        routes.reshape(rows, routes.shape[2]),
        norm_gain,
        jnp.swapaxes(router, 0, 1),
        jnp.swapaxes(gate_w, 1, 2),
        jnp.swapaxes(up_w, 1, 2),
        down_w,
    )


def solution(mesh):
    return jax.shard_map(
        local,
        mesh=mesh,
        in_specs=(
            P("wide", None, "kv"),
            P("wide", None, "kv"),
            P("wide", None, None, "kv"),
            P("kv", "wide", None, None),
            P("kv", "wide", None, None),
            P(),
            P(),
            P(),
            P("wide", None, None),
            P(),
            P(),
            P("wide", None, "kv"),
            P("wide", None, "kv"),
            P("wide", "kv", None),
        ),
        out_specs=P("wide", None, "kv"),
        check_vma=False,
    )
```

```python
import functools
import math

import jax
import jax.numpy as jnp
from jax import lax
from jax.experimental import pallas as pl
from jax.experimental.pallas import tpu as pltpu
from jax.sharding import PartitionSpec as P

MESH = pl.DeviceIdType.MESH
HD = 128
BEAMS = 8
BLK = 128
MOST = 2
F32 = jnp.float32
BF16 = jnp.bfloat16


def far_first(n):
    order = sorted(range(1, n), key=lambda d: -min(d, n - d))
    return order


def near_first(n):
    return sorted(range(1, n), key=lambda d: min(d, n - d))


def rcopy(src, dst, send_sem, recv_sem, device):
    return pltpu.make_async_remote_copy(
        src_ref=src,
        dst_ref=dst,
        send_sem=send_sem,
        recv_sem=recv_sem,
        device_id=device,
        device_id_type=MESH,
    )


def dot(x, y):
    return jnp.dot(x, y, preferred_element_type=F32)


def iota(shape, axis):
    return lax.broadcasted_iota(jnp.int32, shape, axis)


def kernel(
    n,
    kv_count,
    heads,
    stream_ref,
    query_ref,
    newkv_ref,
    keys_hbm,
    values_hbm,
    lengths_ref,
    table_ref,
    parents_ref,
    routes_ref,
    gain_hbm,
    router_hbm,
    gate_hbm,
    up_hbm,
    down_hbm,
    out_ref,
    keys,
    values,
    router,
    gate,
    up,
    down,
    gain,
    load_sem,
    weight_sems,
    query,
    query_parts,
    q_all,
    kvgroup,
    routes_b,
    q_sems,
    slot_group,
    slot_limit,
    slot_prev,
    group_last,
    sums_all,
    part_all,
    sibling_part,
    core_sum_all,
    b_parts,
    b_sum,
    a_parts,
    part_sems,
    resid,
    mid_resid,
    x_sems,
    line_ready,
    mid_perm,
    rows,
    row_sems,
    x_send,
    back_mid,
    back_sum,
    back_rows,
    back_sems,
):
    kv = lax.axis_index("kv")
    w = lax.axis_index("wide")
    c = w % 2
    z = (w // 2) % n
    y = w // (2 * n)
    a = z + c * (y - z)
    b = y + c * (z - y)
    stride_a = 2 + c * (2 * n - 2)
    stride_b = 2 * n - c * (2 * n - 2)
    sib = {"wide": w + 1 - 2 * c}
    width = heads * HD
    row_count = query.shape[0]
    slots = keys.shape[0]
    groups = lengths_ref.shape[0]
    blocks = table_ref.shape[1]
    steps = parents_ref.shape[0] + 1
    top = routes_ref.shape[1]
    units = gate.shape[0] // 2
    w_send, w_recv = weight_sems
    model = kv_count * width
    cols = n * n * MOST
    block_rows = n * MOST
    mids = n * row_count
    scale = 1.0 / math.sqrt(HD)

    def dev_a(j):
        return {"wide": w + (j - a) * stride_a}

    def dev_b(j):
        return {"wide": w + (j - b) * stride_b}

    def dev_xa(i, j):
        return {"kv": i, "wide": w + (j - a) * stride_a}

    def dev_xb(i, j):
        return {"kv": i, "wide": w + (j - b) * stride_b}

    spans = [(0, (heads + 1) // 2), ((heads + 1) // 2, heads)]

    group_first = w // 4 * 4
    group_place = w % 4

    loads = [
        pltpu.make_async_copy(src, dst, load_sem.at[i])
        for i, (src, dst) in enumerate(
            [
                (keys_hbm.at[0], keys),
                (values_hbm.at[0], values),
                (router_hbm, router),
                (gate_hbm.at[0], gate.at[0:units]),
                (up_hbm.at[0], up.at[0:units]),
                (gain_hbm, gain.at[0]),
            ]
            + [
                (down_hbm.at[0, :, i * width : (i + 1) * width], down.at[i, 0:units])
                for i in range(kv_count)
            ]
        )
    ]
    query[...] = query_ref[...].reshape(query.shape)
    for (first, last), share_q, all_q in zip(spans, query_parts, q_all):
        share_q[...] = query[:, first * HD : last * HD]
        all_q[c, b, a] = share_q[...]
    kvgroup[group_place] = newkv_ref[...].reshape(row_count, 2 * HD)
    routes_b[b] = routes_ref[...]

    barrier = pltpu.get_barrier_semaphore()
    greeted = 0
    for d in far_first(n):
        for device in (dev_a((a + d) % n), dev_b((b + d) % n)):
            pl.semaphore_signal(barrier, inc=1, device_id=device, device_id_type=MESH)
            greeted += 1
    kv_peers = [{"kv": (kv + d) % kv_count} for d in range(1, kv_count)]
    for device in kv_peers:
        pl.semaphore_signal(barrier, inc=1, device_id=device, device_id_type=MESH)
        greeted += 1
    for d in range(1, 4):
        pl.semaphore_signal(
            barrier,
            inc=1,
            device_id={"wide": group_first + (group_place + d) % 4},
            device_id_type=MESH,
        )
        greeted += 1
    pl.semaphore_wait(barrier, greeted)

    sent = []

    def send(copy):
        copy.start()
        sent.append(copy)

    q_send, q_recv = q_sems
    for ch, share_q in enumerate(query_parts):
        for d in far_first(n):
            send(
                rcopy(
                    share_q,
                    q_all[ch].at[c, b, a],
                    q_send.at[7 * ch, d],
                    q_recv.at[7 * ch, a],
                    dev_a((a + d) % n),
                )
            )
    for load in loads[:2]:
        load.start()
    for device in kv_peers:
        pl.semaphore_signal(line_ready, inc=1, device_id=device, device_id_type=MESH)
    for d in range(1, 4):
        peer = group_first + (group_place + d) % 4
        send(
            rcopy(
                kvgroup.at[group_place],
                kvgroup.at[group_place],
                q_send.at[3, d],
                q_recv.at[3, group_place],
                {"wide": peer},
            )
        )

    for ch in range(2):
        for d in near_first(n):
            j = (a + d) % n
            rcopy(
                query_parts[ch], q_all[ch].at[c, b, j], q_send.at[7 * ch, d], q_recv.at[7 * ch, j], dev_a(j)
            ).wait_recv()
        block = q_all[ch].at[c, b]
        for d in far_first(n):
            send(
                rcopy(
                    block, block, q_send.at[1 + 4 * ch, d], q_recv.at[1 + 4 * ch, b], dev_b((b + d) % n)
                )
            )
        send(rcopy(block, block, q_send.at[2 + 4 * ch, 0], q_recv.at[2 + 4 * ch, b], sib))
    for d in far_first(n):
        send(
            rcopy(
                routes_b.at[b],
                routes_b.at[b],
                q_send.at[4, d],
                q_recv.at[4, b],
                dev_b((b + d) % n),
            )
        )

    for load in loads[2:]:
        load.start()

    table = table_ref[...]
    place = iota((groups, blocks), 0) * blocks + iota((groups, blocks), 1) + 1
    owners = []
    for s in range(slots):
        code = jnp.max(jnp.where(table == w * slots + s, place, 0))
        live = jnp.minimum(code, 1)
        spot = jnp.maximum(code - 1, 0)
        group = spot // blocks
        slot_group[s] = group
        slot_limit[s] = live * (lengths_ref[group] - spot % blocks * BLK)
        owners.append(jnp.where(code > 0, group, -1))
    for s in range(slots):
        before = jnp.int32(slots)
        for r in range(s):
            before = jnp.where(owners[r] == owners[s], r, before)
        slot_prev[s] = before
    for g in range(groups):
        last = jnp.int32(slots)
        for s in range(slots):
            last = jnp.where(owners[s] == g, s, last)
        group_last[g] = last

    def pass_on(ch):
        for d in near_first(n):
            j = (b + d) % n
            block = q_all[ch].at[c, j]
            rcopy(
                block, block, q_send.at[1 + 4 * ch, d], q_recv.at[1 + 4 * ch, j], dev_b(j)
            ).wait_recv()
            send(rcopy(block, block, q_send.at[2 + 4 * ch, d], q_recv.at[2 + 4 * ch, j], sib))

    def await_sibling(ch):
        for j in range(n):
            block = q_all[ch].at[1 - c, j]
            rcopy(
                block, block, q_send.at[2 + 4 * ch, j], q_recv.at[2 + 4 * ch, j], sib
            ).wait_recv()

    half_n = n // 2
    group_rows = 4 * row_count
    lane = iota((row_count, HD), 1)
    p_send, p_recv = part_sems

    def attend(ch):
        first_head, last_head = spans[ch]
        count = last_head - first_head
        sums, part = sums_all[ch], part_all[ch]
        tiles = n * count
        qfull = q_all[ch]

        def one_slot(s):
            group = slot_group[s]
            gy = group // half_n
            gz = group % half_n * 2
            q = jnp.concatenate(
                [
                    qfull[0, gy, gz],
                    qfull[0, gy, gz + 1],
                    qfull[1, gz, gy],
                    qfull[1, gz + 1, gy],
                ],
                axis=0,
            )
            q = jnp.concatenate([q[:, r * HD : (r + 1) * HD] for r in range(count)], axis=0)
            scores = lax.dot_general(
                q, keys[s], (((1,), (1,)), ((), ())), preferred_element_type=F32
            )
            ok = iota(scores.shape, 1) < slot_limit[s]
            weights = jnp.where(ok, jnp.exp(scores * scale), 0.0).astype(BF16)
            extended = jnp.concatenate([values[s], jnp.ones((BLK, HD), BF16)], axis=1)
            sums[s] = dot(weights, extended)

        def slot_block(s, carry):
            for i in range(4):
                one_slot(s * 4 + i)
            return carry

        sums[slots] = jnp.zeros(sums.shape[1:], F32)
        lax.fori_loop(0, slots // 4, slot_block, 0)

        def link_slot(s, carry):
            sums[s] = sums[s] + sums[slot_prev[s]]
            return carry

        lax.fori_loop(0, slots, link_slot, 0)

        for core in range(2):
            for j in range(n):
                part[core, j, tiles] = jnp.zeros((row_count, HD), BF16)

        def one_group(g, carry):
            last = group_last[g]
            gy = g // half_n
            gz = g % half_n * 2
            for core in range(2):
                for zl in range(2):
                    bi, ai = (gy, gz + zl) if core == 0 else (gz + zl, gy)
                    dens = jnp.zeros((row_count, HD), F32)
                    for r in range(count):
                        first = r * group_rows + (core * 2 + zl) * row_count
                        block = sums[last, pl.ds(first, row_count), :]
                        part[core, bi, ai * count + r] = block[:, :HD].astype(BF16)
                        dens = jnp.where(lane % 8 == r, block[:, HD:], dens)
                    old = part[core, bi, tiles].astype(F32)
                    part[core, bi, tiles] = jnp.where(lane // 8 == ai, dens, old).astype(BF16)
            return carry

        lax.fori_loop(0, groups, one_group, 0)
        for d in far_first(n) + [0]:
            j = (a + d) % n
            send(
                rcopy(
                    part.at[1 - c, j],
                    sibling_part[ch].at[j],
                    p_send.at[3 * ch, d],
                    p_recv.at[3 * ch, j],
                    sib,
                )
            )

    def sum_cores(ch):
        part, core_sum = part_all[ch], core_sum_all[ch]
        for d in far_first(n) + [0]:
            j = (b + d) % n
            rcopy(
                part.at[1 - c, j],
                sibling_part[ch].at[j],
                p_send.at[3 * ch, d],
                p_recv.at[3 * ch, j],
                sib,
            ).wait_recv()
            core_sum[j] = (part[c, j].astype(F32) + sibling_part[ch][j].astype(F32)).astype(BF16)
            if d:
                send(
                    rcopy(
                        core_sum.at[j],
                        b_parts[ch].at[b],
                        p_send.at[3 * ch + 1, d],
                        p_recv.at[3 * ch + 1, b],
                        dev_b(j),
                    )
                )

    for j in range(1, 4):
        p = (group_place + j) % 4
        rcopy(
            kvgroup.at[p], kvgroup.at[p], q_send.at[3, j], q_recv.at[3, p], {"wide": group_first + p}
        ).wait_recv()
    key_rows = 4 * row_count
    tail_kv = jnp.concatenate([kvgroup[i] for i in range(4)], axis=0)
    row_id = iota((row_count, key_rows), 0)
    key_id = iota((row_count, key_rows), 1)
    wanted = jnp.full((row_count, key_rows), -1, jnp.int32)
    token_base = w // 4 * BEAMS
    for i in range(row_count // steps):
        for s in range(steps):
            beam = group_place * (row_count // steps) + i
            for j in range(s, -1, -1):
                wanted = jnp.where(
                    (row_id == i * steps + s) & (key_id % steps == j), beam, wanted
                )
                if j:
                    beam = parents_ref[j - 1, token_base + beam]
    allowed = wanted == key_id // steps
    tail_q = jnp.concatenate([query[:, r * HD : (r + 1) * HD] for r in range(heads)], axis=0)
    tail_scores = lax.dot_general(
        tail_q, tail_kv[:, :HD], (((1,), (1,)), ((), ())), preferred_element_type=F32
    )
    tail_ok = jnp.concatenate([allowed.astype(F32)] * heads, axis=0)
    tail_w = jnp.where(tail_ok > 0, jnp.exp(tail_scores * scale), 0.0).astype(BF16)
    tail_num = dot(tail_w, tail_kv[:, HD:])
    tail_den = jnp.sum(tail_w.astype(F32), axis=1, keepdims=True)

    pass_on(0)
    await_sibling(0)
    loads[0].wait()
    loads[1].wait()
    attend(0)
    pass_on(1)
    sum_cores(0)
    await_sibling(1)
    attend(1)
    sum_cores(1)

    for load in loads[3:5] + loads[6:]:
        load.wait()
    halves = [(gate, 0), (up, 1), (down, 2)]
    for weight, i in halves:
        rows_of = (slice(None),) * (len(weight.shape) - 2)
        send(
            rcopy(
                weight.at[rows_of + (pl.ds(0, units),)],
                weight.at[rows_of + (pl.ds(units, units),)],
                w_send.at[i],
                w_recv.at[i],
                sib,
            )
        )

    for ch, (first_head, last_head) in enumerate(spans):
        count = last_head - first_head
        core_sum, part_b, sum_b = core_sum_all[ch], b_parts[ch], b_sum[ch]
        for d in near_first(n):
            j = (b + d) % n
            rcopy(
                core_sum.at[j], part_b.at[j], p_send.at[3 * ch + 1, d], p_recv.at[3 * ch + 1, j], dev_b(j)
            ).wait_recv()
        dens = core_sum[b, n * count].astype(F32)
        for e in range(1, n):
            dens = dens + part_b[(b + e) % n, n * count].astype(F32)
        dens = dens.astype(BF16)
        for d in far_first(n) + [0]:
            j = (a + d) % n
            chunk = pl.ds(j * count, count)
            total = core_sum[b, chunk].astype(F32)
            for e in range(1, n):
                total = total + part_b[(b + e) % n, chunk].astype(F32)
            sum_b[j, 0:count] = total.astype(BF16)
            sum_b[j, count] = dens
            if d:
                send(
                    rcopy(
                        sum_b.at[j],
                        a_parts[ch].at[a],
                        p_send.at[3 * ch + 2, d],
                        p_recv.at[3 * ch + 2, a],
                        dev_a(j),
                    )
                )
    nums = []
    dens = []
    for ch, (first_head, last_head) in enumerate(spans):
        count = last_head - first_head
        total = b_sum[ch][a].astype(F32)
        for d in near_first(n):
            j = (a + d) % n
            rcopy(
                b_sum[ch].at[j], a_parts[ch].at[j], p_send.at[3 * ch + 2, d], p_recv.at[3 * ch + 2, j], dev_a(j)
            ).wait_recv()
            total = total + a_parts[ch][j].astype(F32)
        for r in range(count):
            nums.append(total[r])
            mine = jnp.where(lane == a * 8 + r, total[count], 0.0)
            dens.append(jnp.sum(mine, axis=1, keepdims=True))

    attended = []
    for r in range(heads):
        num = nums[r] + tail_num[r * row_count : (r + 1) * row_count]
        den = dens[r] + tail_den[r * row_count : (r + 1) * row_count]
        attended.append((num / den).astype(BF16).astype(F32))
    residual = (stream_ref[...].reshape(row_count, width).astype(F32) + jnp.concatenate(attended, axis=1)).astype(BF16)
    resid[...] = residual

    x_ssem, x_rsem = x_sems
    pl.semaphore_wait(line_ready, kv_count - 1)
    spots = [(dx, d) for d in far_first(n) + [0] for dx in far_first(kv_count) + [0]]
    for dx, d in spots[:-1]:
        device = dev_xb((kv + dx) % kv_count, (b + d) % n)
        send(
            rcopy(
                resid,
                mid_resid.at[b, kv],
                x_ssem.at[0, dx * n + d],
                x_rsem.at[0, kv * n + b],
                device,
            )
        )
    mid_resid[b, kv] = residual
    for d in near_first(n):
        j = (b + d) % n
        rcopy(
            routes_b.at[j], routes_b.at[j], q_send.at[4, d], q_recv.at[4, j], dev_b(j)
        ).wait_recv()
    routed = jnp.concatenate([routes_b[j] for j in range(n)], axis=0)
    col = iota((1, cols), 1)
    col_chip = col // block_rows
    col_source = col // MOST % n
    col_place = col % MOST
    col_expert = b * n + col_chip + c * ((col_chip - b) * (n - 1))
    experts = n * n
    source = iota((mids, 1), 0) // row_count
    expert_lane = iota((1, experts), 1)
    hit = jnp.zeros((mids, cols), F32)
    chosen = jnp.zeros((mids, experts), F32)
    for i in range(top):
        hit = jnp.where(routed[:, i : i + 1] == col_expert, 1.0, hit)
        chosen = jnp.where(routed[:, i : i + 1] == expert_lane, 1.0, chosen)
    hit = jnp.where(source == col_source, hit, 0.0)
    first_id = iota((mids, mids), 0)
    second_id = iota((mids, mids), 1)
    earlier = (first_id > second_id) & (first_id // row_count == second_id // row_count)
    taken = dot(earlier.astype(F32).astype(BF16), hit.astype(BF16))
    pick = jnp.where(taken == col_place.astype(F32), hit, 0.0)
    pick_t = jnp.transpose(pick).astype(BF16)
    spread = (iota((experts, cols), 0) == col_expert).astype(F32)

    loads[2].wait()
    loads[5].wait()
    for dx, d in reversed(spots[:-1]):
        i, j = (kv + dx) % kv_count, (b + d) % n
        rcopy(
            resid, mid_resid.at[j, i], x_ssem.at[0, dx * n + d], x_rsem.at[0, i * n + j], dev_xb(i, j)
        ).wait_recv()
    full = jnp.concatenate(
        [
            jnp.concatenate([mid_resid[j, i] for j in range(n)], axis=0).astype(F32)
            for i in range(kv_count)
        ],
        axis=1,
    )
    mean_square = jnp.sum(full * full, axis=1, keepdims=True) / model
    mid = (full * lax.rsqrt(mean_square + 1e-06) * gain[...]).astype(BF16)

    r_send, r_recv = row_sems
    mid_perm[...] = dot(pick_t, mid).astype(BF16).reshape(mid_perm.shape)
    for d in far_first(n):
        j = (a + d) % n
        send(rcopy(mid_perm.at[j], rows.at[a], r_send.at[d], r_recv.at[a], dev_a(j)))
    rows[a] = mid_perm[a]

    logits = lax.dot_general(
        mid, router[...], (((1,), (1,)), ((), ())), preferred_element_type=F32
    )
    col_logits = lax.dot_general(
        logits,
        spread,
        (((1,), (0,)), ((), ())),
        preferred_element_type=F32,
        precision=lax.Precision.HIGHEST,
    )
    raised = jnp.where(chosen > 0, jnp.exp(jnp.where(chosen > 0, logits, 0.0)), 0.0)
    raised_sum = jnp.sum(raised, axis=1, keepdims=True)
    share = jnp.where(pick > 0, jnp.exp(jnp.where(pick > 0, col_logits, 0.0)), 0.0) / raised_sum
    share_high = share.astype(BF16)
    share_low = (share - share_high.astype(F32)).astype(BF16)

    for weight, i in halves:
        rows_of = (slice(None),) * (len(weight.shape) - 2)
        half = weight.at[rows_of + (pl.ds(units, units),)]
        rcopy(half, half, w_send.at[i], w_recv.at[i], sib).wait_recv()
    for d in near_first(n):
        j = (a + d) % n
        rcopy(mid_perm.at[j], rows.at[j], r_send.at[d], r_recv.at[j], dev_a(j)).wait_recv()
    x = rows[...].reshape(cols, model)
    turned = (((1,), (1,)), ((), ()))
    gated = lax.dot_general(x, gate[...], turned, preferred_element_type=F32)
    lifted = lax.dot_general(x, up[...], turned, preferred_element_type=F32)
    hidden = (gated / (1.0 + jnp.exp(-gated)) * lifted).astype(BF16)
    e_send, e_recv = back_sems
    for d in far_first(kv_count) + [0]:
        i = (kv + d) % kv_count
        x_send[i] = dot(hidden, down[i]).astype(BF16).reshape(x_send.shape[1:])
        for da in far_first(n) + [0]:
            j = (a + da) % n
            if d or da:
                send(
                    rcopy(
                        x_send.at[i, j],
                        back_mid.at[kv, a],
                        x_ssem.at[1, d * n + da],
                        x_rsem.at[1, kv * n + a],
                        dev_xa(i, j),
                    )
                )
    back_mid[kv, a] = x_send[kv, a]

    shares = [jnp.concatenate([part] * kv_count, axis=1) for part in (share_high, share_low)]
    for dx, d in [(dx, d) for d in [0] + near_first(n) for dx in range(kv_count)][1:]:
        i, j = (kv + dx) % kv_count, (a + d) % n
        rcopy(
            x_send.at[i, j], back_mid.at[i, j], x_ssem.at[1, dx * n + d], x_rsem.at[1, i * n + j], dev_xa(i, j)
        ).wait_recv()
    returned = back_mid[...].reshape(kv_count * cols, width)
    weighted = dot(shares[0], returned) + dot(shares[1], returned)
    back_sum[...] = weighted.astype(BF16).reshape(back_sum.shape)
    for d in far_first(n):
        j = (b + d) % n
        send(rcopy(back_sum.at[j], back_rows.at[b], e_send.at[d], e_recv.at[b], dev_b(j)))
    combined = resid[...].astype(F32) + back_sum[b].astype(F32)
    for d in near_first(n):
        j = (b + d) % n
        rcopy(
            back_sum.at[j], back_rows.at[j], e_send.at[d], e_recv.at[j], dev_b(j)
        ).wait_recv()
        combined = combined + back_rows[j].astype(F32)
    out_ref[...] = combined.astype(BF16).reshape(out_ref.shape)
    for copy in sent:
        copy.wait_send()


def local(
    stream_in,
    queries,
    new_kv,
    cache_keys,
    cache_values,
    lengths,
    page_table,
    parents,
    routes,
    norm_gain,
    router,
    gate_w,
    up_w,
    down_w,
):
    kv_count = lax.axis_size("kv")
    n = math.isqrt(lax.axis_size("wide") // 2)
    step_tok, steps, width = queries.shape
    rows = step_tok * steps
    heads = width // HD
    slots = cache_keys.shape[1]
    groups = lengths.shape[0]
    model = router.shape[0]
    units = gate_w.shape[2]
    cols = n * n * MOST
    block = n * MOST
    spans = [(heads + 1) // 2, heads // 2]
    per_span = lambda shape, dtype: [vmem(shape(count), dtype) for count in spans]
    dma = pltpu.SemaphoreType.DMA
    vmem = pltpu.VMEM
    sems = lambda stages: (dma((stages, max(n, 4))), dma((stages, max(n, 4))))
    in_vmem = pl.BlockSpec(memory_space=pltpu.VMEM)
    in_smem = pl.BlockSpec(memory_space=pltpu.SMEM)
    in_hbm = pl.BlockSpec(memory_space=pl.ANY)
    return pl.pallas_call(
        functools.partial(kernel, n, kv_count, heads),
        out_shape=jax.ShapeDtypeStruct(stream_in.shape, BF16),
        in_specs=[in_vmem] * 3
        + [in_hbm] * 2
        + [in_smem, in_vmem, in_smem, in_vmem]
        + [in_hbm] * 5,
        out_specs=in_vmem,
        scratch_shapes=[
            vmem((slots, BLK, HD), BF16),
            vmem((slots, BLK, HD), BF16),
            vmem((router.shape[1], model), BF16),
            vmem((2 * units, model), BF16),
            vmem((2 * units, model), BF16),
            vmem((kv_count, 2 * units, width), BF16),
            vmem((1, model), F32),
            dma((6 + kv_count,)),
            (dma((3,)), dma((3,))),
            vmem((rows, width), BF16),
            per_span(lambda k: (rows, k * HD), BF16),
            per_span(lambda k: (2, n, n, rows, k * HD), BF16),
            vmem((4, rows, 2 * HD), BF16),
            vmem((n, rows, routes.shape[2]), jnp.int32),
            sems(8),
            pltpu.SMEM((slots,), jnp.int32),
            pltpu.SMEM((slots,), jnp.int32),
            pltpu.SMEM((slots,), jnp.int32),
            pltpu.SMEM((groups,), jnp.int32),
            per_span(lambda k: (slots + 1, 4 * rows * k, 2 * HD), F32),
            per_span(lambda k: (2, n, n * k + 1, rows, HD), BF16),
            per_span(lambda k: (n, n * k + 1, rows, HD), BF16),
            per_span(lambda k: (n, n * k + 1, rows, HD), BF16),
            per_span(lambda k: (n, n * k + 1, rows, HD), BF16),
            per_span(lambda k: (n, k + 1, rows, HD), BF16),
            per_span(lambda k: (n, k + 1, rows, HD), BF16),
            sems(6),
            vmem((rows, width), BF16),
            vmem((n, kv_count, rows, width), BF16),
            (dma((2, kv_count * n)), dma((2, kv_count * n))),
            pltpu.SemaphoreType.REGULAR,
            vmem((n, block, model), BF16),
            vmem((n, block, model), BF16),
            (dma((n,)), dma((n,))),
            vmem((kv_count, n, block, width), BF16),
            vmem((kv_count, n, block, width), BF16),
            vmem((n, rows, width), BF16),
            vmem((n, rows, width), BF16),
            (dma((n,)), dma((n,))),
        ],
        compiler_params=pltpu.CompilerParams(collective_id=0, has_side_effects=True),
        name="layer",
    )(
        stream_in,
        queries,
        new_kv,
        cache_keys,
        cache_values,
        lengths,
        page_table,
        jnp.swapaxes(parents, 0, 1),
        routes.reshape(rows, routes.shape[2]),
        norm_gain,
        jnp.swapaxes(router, 0, 1),
        jnp.swapaxes(gate_w, 1, 2),
        jnp.swapaxes(up_w, 1, 2),
        down_w,
    )


def solution(mesh):
    return jax.shard_map(
        local,
        mesh=mesh,
        in_specs=(
            P("wide", None, "kv"),
            P("wide", None, "kv"),
            P("wide", None, None, "kv"),
            P("kv", "wide", None, None),
            P("kv", "wide", None, None),
            P(),
            P(),
            P(),
            P("wide", None, None),
            P(),
            P(),
            P("wide", None, "kv"),
            P("wide", None, "kv"),
            P("wide", "kv", None),
        ),
        out_specs=P("wide", None, "kv"),
        check_vma=False,
    )
```

```python
import functools
import math

import jax
import jax.numpy as jnp
from jax import lax
from jax.experimental import pallas as pl
from jax.experimental.pallas import tpu as pltpu
from jax.sharding import PartitionSpec as P

MESH = pl.DeviceIdType.MESH
HD = 128
BEAMS = 8
BLK = 128
MOST = 2
F32 = jnp.float32
BF16 = jnp.bfloat16


def far_first(n):
    order = sorted(range(1, n), key=lambda d: -min(d, n - d))
    return order


def near_first(n):
    return sorted(range(1, n), key=lambda d: min(d, n - d))


def rcopy(src, dst, send_sem, recv_sem, device):
    return pltpu.make_async_remote_copy(
        src_ref=src,
        dst_ref=dst,
        send_sem=send_sem,
        recv_sem=recv_sem,
        device_id=device,
        device_id_type=MESH,
    )


def dot(x, y):
    return jnp.dot(x, y, preferred_element_type=F32)


def iota(shape, axis):
    return lax.broadcasted_iota(jnp.int32, shape, axis)


def kernel(
    n,
    kv_count,
    heads,
    stream_ref,
    query_ref,
    newkv_ref,
    keys_hbm,
    values_hbm,
    lengths_ref,
    table_ref,
    parents_ref,
    routes_ref,
    gain_hbm,
    router_hbm,
    gate_hbm,
    up_hbm,
    down_hbm,
    out_ref,
    keys,
    values,
    router,
    gate,
    up,
    down,
    gain,
    load_sem,
    weight_sems,
    query,
    query_parts,
    q_all,
    kvgroup,
    routes_b,
    q_sems,
    slot_group,
    slot_limit,
    slot_prev,
    group_last,
    sums_all,
    part_all,
    sibling_part,
    core_sum_all,
    b_parts,
    b_sum,
    a_parts,
    part_sems,
    resid,
    mid_resid,
    x_sems,
    line_ready,
    mid_perm,
    rows,
    row_sems,
    x_send,
    back_mid,
    back_sum,
    back_rows,
    back_sems,
):
    kv = lax.axis_index("kv")
    w = lax.axis_index("wide")
    c = w % 2
    z = (w // 2) % n
    y = w // (2 * n)
    a = z + c * (y - z)
    b = y + c * (z - y)
    stride_a = 2 + c * (2 * n - 2)
    stride_b = 2 * n - c * (2 * n - 2)
    sib = {"wide": w + 1 - 2 * c}
    width = heads * HD
    row_count = query.shape[0]
    slots = keys.shape[0]
    groups = lengths_ref.shape[0]
    blocks = table_ref.shape[1]
    steps = parents_ref.shape[0] + 1
    top = routes_ref.shape[1]
    units = gate.shape[0] // 2
    w_send, w_recv = weight_sems
    model = kv_count * width
    cols = n * n * MOST
    block_rows = n * MOST
    mids = n * row_count
    half_cols = cols // 2
    half_rows = block_rows // 2
    scale = 1.0 / math.sqrt(HD)

    def dev_a(j):
        return {"wide": w + (j - a) * stride_a}

    def dev_b(j):
        return {"wide": w + (j - b) * stride_b}

    def dev_xa(i, j):
        return {"kv": i, "wide": w + (j - a) * stride_a}

    def dev_xb(i, j):
        return {"kv": i, "wide": w + (j - b) * stride_b}

    spans = [(0, (heads + 1) // 2), ((heads + 1) // 2, heads)]

    group_first = w // 4 * 4
    group_place = w % 4

    loads = [
        pltpu.make_async_copy(src, dst, load_sem.at[i])
        for i, (src, dst) in enumerate(
            [
                (keys_hbm.at[0], keys),
                (values_hbm.at[0], values),
                (router_hbm, router),
                (gate_hbm.at[0], gate.at[0:units]),
                (up_hbm.at[0], up.at[0:units]),
                (gain_hbm, gain.at[0]),
            ]
            + [
                (down_hbm.at[0, :, i * width : (i + 1) * width], down.at[i, 0:units])
                for i in range(kv_count)
            ]
        )
    ]
    query[...] = query_ref[...].reshape(query.shape)
    for (first, last), share_q, all_q in zip(spans, query_parts, q_all):
        share_q[...] = query[:, first * HD : last * HD]
        all_q[c, b, a] = share_q[...]
    kvgroup[group_place] = newkv_ref[...].reshape(row_count, 2 * HD)
    routes_b[b] = routes_ref[...]

    barrier = pltpu.get_barrier_semaphore()
    greeted = 0
    for d in far_first(n):
        for device in (dev_a((a + d) % n), dev_b((b + d) % n)):
            pl.semaphore_signal(barrier, inc=1, device_id=device, device_id_type=MESH)
            greeted += 1
    kv_peers = [{"kv": (kv + d) % kv_count} for d in range(1, kv_count)]
    for device in kv_peers:
        pl.semaphore_signal(barrier, inc=1, device_id=device, device_id_type=MESH)
        greeted += 1
    for d in range(1, 4):
        pl.semaphore_signal(
            barrier,
            inc=1,
            device_id={"wide": group_first + (group_place + d) % 4},
            device_id_type=MESH,
        )
        greeted += 1
    pl.semaphore_wait(barrier, greeted)

    sent = []

    def send(copy):
        copy.start()
        sent.append(copy)

    q_send, q_recv = q_sems
    for ch, share_q in enumerate(query_parts):
        for d in far_first(n):
            send(
                rcopy(
                    share_q,
                    q_all[ch].at[c, b, a],
                    q_send.at[7 * ch, d],
                    q_recv.at[7 * ch, a],
                    dev_a((a + d) % n),
                )
            )
    for load in loads[:2]:
        load.start()
    for device in kv_peers:
        pl.semaphore_signal(line_ready, inc=1, device_id=device, device_id_type=MESH)
    for d in range(1, 4):
        peer = group_first + (group_place + d) % 4
        send(
            rcopy(
                kvgroup.at[group_place],
                kvgroup.at[group_place],
                q_send.at[3, d],
                q_recv.at[3, group_place],
                {"wide": peer},
            )
        )

    for ch in range(2):
        for d in near_first(n):
            j = (a + d) % n
            rcopy(
                query_parts[ch], q_all[ch].at[c, b, j], q_send.at[7 * ch, d], q_recv.at[7 * ch, j], dev_a(j)
            ).wait_recv()
        block = q_all[ch].at[c, b]
        for d in far_first(n):
            send(
                rcopy(
                    block, block, q_send.at[1 + 4 * ch, d], q_recv.at[1 + 4 * ch, b], dev_b((b + d) % n)
                )
            )
        send(rcopy(block, block, q_send.at[2 + 4 * ch, 0], q_recv.at[2 + 4 * ch, b], sib))
    for d in far_first(n):
        send(
            rcopy(
                routes_b.at[b],
                routes_b.at[b],
                q_send.at[4, d],
                q_recv.at[4, b],
                dev_b((b + d) % n),
            )
        )

    for load in loads[2:]:
        load.start()

    table = table_ref[...]
    place = iota((groups, blocks), 0) * blocks + iota((groups, blocks), 1) + 1
    owners = []
    for s in range(slots):
        code = jnp.max(jnp.where(table == w * slots + s, place, 0))
        live = jnp.minimum(code, 1)
        spot = jnp.maximum(code - 1, 0)
        group = spot // blocks
        slot_group[s] = group
        slot_limit[s] = live * (lengths_ref[group] - spot % blocks * BLK)
        owners.append(jnp.where(code > 0, group, -1))
    for s in range(slots):
        before = jnp.int32(slots)
        for r in range(s):
            before = jnp.where(owners[r] == owners[s], r, before)
        slot_prev[s] = before
    for g in range(groups):
        last = jnp.int32(slots)
        for s in range(slots):
            last = jnp.where(owners[s] == g, s, last)
        group_last[g] = last

    def pass_on(ch):
        for d in near_first(n):
            j = (b + d) % n
            block = q_all[ch].at[c, j]
            rcopy(
                block, block, q_send.at[1 + 4 * ch, d], q_recv.at[1 + 4 * ch, j], dev_b(j)
            ).wait_recv()
            send(rcopy(block, block, q_send.at[2 + 4 * ch, d], q_recv.at[2 + 4 * ch, j], sib))

    def await_sibling(ch):
        for j in range(n):
            block = q_all[ch].at[1 - c, j]
            rcopy(
                block, block, q_send.at[2 + 4 * ch, j], q_recv.at[2 + 4 * ch, j], sib
            ).wait_recv()

    half_n = n // 2
    group_rows = 4 * row_count
    lane = iota((row_count, HD), 1)
    p_send, p_recv = part_sems

    def attend(ch):
        first_head, last_head = spans[ch]
        count = last_head - first_head
        sums, part = sums_all[ch], part_all[ch]
        tiles = n * count
        qfull = q_all[ch]

        def one_slot(s):
            group = slot_group[s]
            gy = group // half_n
            gz = group % half_n * 2
            q = jnp.concatenate(
                [
                    qfull[0, gy, gz],
                    qfull[0, gy, gz + 1],
                    qfull[1, gz, gy],
                    qfull[1, gz + 1, gy],
                ],
                axis=0,
            )
            q = jnp.concatenate([q[:, r * HD : (r + 1) * HD] for r in range(count)], axis=0)
            scores = lax.dot_general(
                q, keys[s], (((1,), (1,)), ((), ())), preferred_element_type=F32
            )
            ok = iota(scores.shape, 1) < slot_limit[s]
            weights = jnp.where(ok, jnp.exp(scores * scale), 0.0).astype(BF16)
            extended = jnp.concatenate([values[s], jnp.ones((BLK, HD), BF16)], axis=1)
            sums[s] = dot(weights, extended)

        def slot_block(s, carry):
            for i in range(4):
                one_slot(s * 4 + i)
            return carry

        sums[slots] = jnp.zeros(sums.shape[1:], F32)
        lax.fori_loop(0, slots // 4, slot_block, 0)

        def link_slot(s, carry):
            sums[s] = sums[s] + sums[slot_prev[s]]
            return carry

        lax.fori_loop(0, slots, link_slot, 0)

        for core in range(2):
            for j in range(n):
                part[core, j, tiles] = jnp.zeros((row_count, HD), BF16)

        def one_group(g, carry):
            last = group_last[g]
            gy = g // half_n
            gz = g % half_n * 2
            for core in range(2):
                for zl in range(2):
                    bi, ai = (gy, gz + zl) if core == 0 else (gz + zl, gy)
                    dens = jnp.zeros((row_count, HD), F32)
                    for r in range(count):
                        first = r * group_rows + (core * 2 + zl) * row_count
                        block = sums[last, pl.ds(first, row_count), :]
                        part[core, bi, ai * count + r] = block[:, :HD].astype(BF16)
                        dens = jnp.where(lane % 8 == r, block[:, HD:], dens)
                    old = part[core, bi, tiles].astype(F32)
                    part[core, bi, tiles] = jnp.where(lane // 8 == ai, dens, old).astype(BF16)
            return carry

        lax.fori_loop(0, groups, one_group, 0)
        for d in far_first(n) + [0]:
            j = (a + d) % n
            send(
                rcopy(
                    part.at[1 - c, j],
                    sibling_part[ch].at[j],
                    p_send.at[3 * ch, d],
                    p_recv.at[3 * ch, j],
                    sib,
                )
            )

    def sum_cores(ch):
        part, core_sum = part_all[ch], core_sum_all[ch]
        for d in far_first(n) + [0]:
            j = (b + d) % n
            rcopy(
                part.at[1 - c, j],
                sibling_part[ch].at[j],
                p_send.at[3 * ch, d],
                p_recv.at[3 * ch, j],
                sib,
            ).wait_recv()
            core_sum[j] = (part[c, j].astype(F32) + sibling_part[ch][j].astype(F32)).astype(BF16)
            if d:
                send(
                    rcopy(
                        core_sum.at[j],
                        b_parts[ch].at[b],
                        p_send.at[3 * ch + 1, d],
                        p_recv.at[3 * ch + 1, b],
                        dev_b(j),
                    )
                )

    for j in range(1, 4):
        p = (group_place + j) % 4
        rcopy(
            kvgroup.at[p], kvgroup.at[p], q_send.at[3, j], q_recv.at[3, p], {"wide": group_first + p}
        ).wait_recv()
    key_rows = 4 * row_count
    tail_kv = jnp.concatenate([kvgroup[i] for i in range(4)], axis=0)
    row_id = iota((row_count, key_rows), 0)
    key_id = iota((row_count, key_rows), 1)
    wanted = jnp.full((row_count, key_rows), -1, jnp.int32)
    token_base = w // 4 * BEAMS
    for i in range(row_count // steps):
        for s in range(steps):
            beam = group_place * (row_count // steps) + i
            for j in range(s, -1, -1):
                wanted = jnp.where(
                    (row_id == i * steps + s) & (key_id % steps == j), beam, wanted
                )
                if j:
                    beam = parents_ref[j - 1, token_base + beam]
    allowed = wanted == key_id // steps
    tail_q = jnp.concatenate([query[:, r * HD : (r + 1) * HD] for r in range(heads)], axis=0)
    tail_scores = lax.dot_general(
        tail_q, tail_kv[:, :HD], (((1,), (1,)), ((), ())), preferred_element_type=F32
    )
    tail_ok = jnp.concatenate([allowed.astype(F32)] * heads, axis=0)
    tail_w = jnp.where(tail_ok > 0, jnp.exp(tail_scores * scale), 0.0).astype(BF16)
    tail_num = dot(tail_w, tail_kv[:, HD:])
    tail_den = jnp.sum(tail_w.astype(F32), axis=1, keepdims=True)

    pass_on(0)
    await_sibling(0)
    loads[0].wait()
    loads[1].wait()
    attend(0)
    pass_on(1)
    sum_cores(0)
    await_sibling(1)
    attend(1)
    sum_cores(1)

    for load in loads[3:5] + loads[6:]:
        load.wait()
    halves = [(gate, 0), (up, 1), (down, 2)]
    for weight, i in halves:
        rows_of = (slice(None),) * (len(weight.shape) - 2)
        send(
            rcopy(
                weight.at[rows_of + (pl.ds(0, units),)],
                weight.at[rows_of + (pl.ds(units, units),)],
                w_send.at[i],
                w_recv.at[i],
                sib,
            )
        )

    for ch, (first_head, last_head) in enumerate(spans):
        count = last_head - first_head
        core_sum, part_b, sum_b = core_sum_all[ch], b_parts[ch], b_sum[ch]
        for d in near_first(n):
            j = (b + d) % n
            rcopy(
                core_sum.at[j], part_b.at[j], p_send.at[3 * ch + 1, d], p_recv.at[3 * ch + 1, j], dev_b(j)
            ).wait_recv()
        dens = core_sum[b, n * count].astype(F32)
        for e in range(1, n):
            dens = dens + part_b[(b + e) % n, n * count].astype(F32)
        dens = dens.astype(BF16)
        for d in far_first(n) + [0]:
            j = (a + d) % n
            chunk = pl.ds(j * count, count)
            total = core_sum[b, chunk].astype(F32)
            for e in range(1, n):
                total = total + part_b[(b + e) % n, chunk].astype(F32)
            sum_b[j, 0:count] = total.astype(BF16)
            sum_b[j, count] = dens
            if d:
                send(
                    rcopy(
                        sum_b.at[j],
                        a_parts[ch].at[a],
                        p_send.at[3 * ch + 2, d],
                        p_recv.at[3 * ch + 2, a],
                        dev_a(j),
                    )
                )
    nums = []
    dens = []
    for ch, (first_head, last_head) in enumerate(spans):
        count = last_head - first_head
        total = b_sum[ch][a].astype(F32)
        for d in near_first(n):
            j = (a + d) % n
            rcopy(
                b_sum[ch].at[j], a_parts[ch].at[j], p_send.at[3 * ch + 2, d], p_recv.at[3 * ch + 2, j], dev_a(j)
            ).wait_recv()
            total = total + a_parts[ch][j].astype(F32)
        for r in range(count):
            nums.append(total[r])
            mine = jnp.where(lane == a * 8 + r, total[count], 0.0)
            dens.append(jnp.sum(mine, axis=1, keepdims=True))

    attended = []
    for r in range(heads):
        num = nums[r] + tail_num[r * row_count : (r + 1) * row_count]
        den = dens[r] + tail_den[r * row_count : (r + 1) * row_count]
        attended.append((num / den).astype(BF16).astype(F32))
    residual = (stream_ref[...].reshape(row_count, width).astype(F32) + jnp.concatenate(attended, axis=1)).astype(BF16)
    resid[...] = residual

    x_ssem, x_rsem = x_sems
    pl.semaphore_wait(line_ready, kv_count - 1)
    spots = [(dx, d) for d in far_first(n) + [0] for dx in far_first(kv_count) + [0]]
    for dx, d in spots[:-1]:
        device = dev_xb((kv + dx) % kv_count, (b + d) % n)
        send(
            rcopy(
                resid,
                mid_resid.at[b, kv],
                x_ssem.at[0, dx * n + d],
                x_rsem.at[0, kv * n + b],
                device,
            )
        )
    mid_resid[b, kv] = residual
    for d in near_first(n):
        j = (b + d) % n
        rcopy(
            routes_b.at[j], routes_b.at[j], q_send.at[4, d], q_recv.at[4, j], dev_b(j)
        ).wait_recv()
    routed = jnp.concatenate([routes_b[(b + p) % n] for p in range(n)], axis=0)
    col = iota((1, cols), 1)
    col_chip = col % half_cols // half_rows
    col_source = col // half_cols * half_n + col // MOST % half_n
    col_place = col % MOST
    col_expert = b * n + col_chip + c * ((col_chip - b) * (n - 1))
    experts = n * n
    source = iota((mids, 1), 0) // row_count
    expert_lane = iota((1, experts), 1)
    hit = jnp.zeros((mids, cols), F32)
    chosen = jnp.zeros((mids, experts), F32)
    for i in range(top):
        hit = jnp.where(routed[:, i : i + 1] == col_expert, 1.0, hit)
        chosen = jnp.where(routed[:, i : i + 1] == expert_lane, 1.0, chosen)
    hit = jnp.where(source == col_source, hit, 0.0)
    first_id = iota((mids, mids), 0)
    second_id = iota((mids, mids), 1)
    earlier = (first_id > second_id) & (first_id // row_count == second_id // row_count)
    taken = dot(earlier.astype(F32).astype(BF16), hit.astype(BF16))
    pick = jnp.where(taken == col_place.astype(F32), hit, 0.0)
    pick_t = jnp.transpose(pick).astype(BF16)
    spread = (iota((experts, cols), 0) == col_expert).astype(F32)

    loads[2].wait()
    loads[5].wait()
    for dx, d in reversed(spots[:-1]):
        i, j = (kv + dx) % kv_count, (b + d) % n
        rcopy(
            resid, mid_resid.at[j, i], x_ssem.at[0, dx * n + d], x_rsem.at[0, i * n + j], dev_xb(i, j)
        ).wait_recv()
    full = jnp.concatenate(
        [
            jnp.concatenate([mid_resid[(b + p) % n, i] for p in range(n)], axis=0).astype(F32)
            for i in range(kv_count)
        ],
        axis=1,
    )
    mean_square = jnp.sum(full * full, axis=1, keepdims=True) / model
    mid = (full * lax.rsqrt(mean_square + 1e-06) * gain[...]).astype(BF16)

    r_send, r_recv = row_sems
    for u in (1, 0):
        picked = dot(pick_t[u * half_cols : (u + 1) * half_cols], mid)
        mid_perm[u] = picked.astype(BF16).reshape(mid_perm.shape[1:])
        for d in far_first(n):
            j = (a + d) % n
            send(
                rcopy(mid_perm.at[u, j], rows.at[u, a], r_send.at[u, d], r_recv.at[u, a], dev_a(j))
            )
        rows[u, a] = mid_perm[u, a]

    logits = lax.dot_general(
        mid, router[...], (((1,), (1,)), ((), ())), preferred_element_type=F32
    )
    col_logits = lax.dot_general(
        logits,
        spread,
        (((1,), (0,)), ((), ())),
        preferred_element_type=F32,
        precision=lax.Precision.HIGHEST,
    )
    raised = jnp.where(chosen > 0, jnp.exp(jnp.where(chosen > 0, logits, 0.0)), 0.0)
    raised_sum = jnp.sum(raised, axis=1, keepdims=True)
    share = jnp.where(pick > 0, jnp.exp(jnp.where(pick > 0, col_logits, 0.0)), 0.0) / raised_sum
    share_high = share.astype(BF16)
    share_low = (share - share_high.astype(F32)).astype(BF16)

    for weight, i in halves:
        rows_of = (slice(None),) * (len(weight.shape) - 2)
        half = weight.at[rows_of + (pl.ds(units, units),)]
        rcopy(half, half, w_send.at[i], w_recv.at[i], sib).wait_recv()
    turned = (((1,), (1,)), ((), ()))
    for u in (1, 0):
        for d in near_first(n):
            j = (a + d) % n
            rcopy(
                mid_perm.at[u, j], rows.at[u, j], r_send.at[u, d], r_recv.at[u, j], dev_a(j)
            ).wait_recv()
        x = rows[u].reshape(half_cols, model)
        gated = lax.dot_general(x, gate[...], turned, preferred_element_type=F32)
        lifted = lax.dot_general(x, up[...], turned, preferred_element_type=F32)
        hidden = (gated / (1.0 + jnp.exp(-gated)) * lifted).astype(BF16)
        for d in far_first(kv_count) + [0]:
            i = (kv + d) % kv_count
            x_send[u, i] = dot(hidden, down[i]).astype(BF16).reshape(x_send.shape[2:])
            for da in far_first(n) + [0]:
                j = (a + da) % n
                if d or da:
                    send(
                        rcopy(
                            x_send.at[u, i, j],
                            back_mid.at[u, kv, a],
                            x_ssem.at[1 + u, d * n + da],
                            x_rsem.at[1 + u, kv * n + a],
                            dev_xa(i, j),
                        )
                    )
        back_mid[u, kv, a] = x_send[u, kv, a]

    e_send, e_recv = back_sems
    half_mids = mids // 2
    for u in (1, 0):
        own_rows = slice(u * half_mids, (u + 1) * half_mids)
        own_cols = slice(u * half_cols, (u + 1) * half_cols)
        shares = [
            jnp.concatenate([part[own_rows, own_cols]] * kv_count, axis=1)
            for part in (share_high, share_low)
        ]
        for dx, d in [(dx, d) for d in [0] + near_first(n) for dx in range(kv_count)][1:]:
            i, j = (kv + dx) % kv_count, (a + d) % n
            rcopy(
                x_send.at[u, i, j],
                back_mid.at[u, i, j],
                x_ssem.at[1 + u, dx * n + d],
                x_rsem.at[1 + u, i * n + j],
                dev_xa(i, j),
            ).wait_recv()
        returned = back_mid[u].reshape(kv_count * half_cols, width)
        weighted = dot(shares[0], returned) + dot(shares[1], returned)
        back_sum[u * half_n : (u + 1) * half_n] = weighted.astype(BF16).reshape((half_n,) + back_sum.shape[1:])
        for p in far_first(n):
            if p // half_n == u:
                send(
                    rcopy(
                        back_sum.at[p], back_rows.at[b], e_send.at[p], e_recv.at[b], dev_b((b + p) % n)
                    )
                )
    combined = resid[...].astype(F32) + back_sum[0].astype(F32)
    for d in near_first(n):
        j = (b + d) % n
        rcopy(
            back_sum.at[d], back_rows.at[j], e_send.at[d], e_recv.at[j], dev_b(j)
        ).wait_recv()
        combined = combined + back_rows[j].astype(F32)
    out_ref[...] = combined.astype(BF16).reshape(out_ref.shape)
    for copy in sent:
        copy.wait_send()


def local(
    stream_in,
    queries,
    new_kv,
    cache_keys,
    cache_values,
    lengths,
    page_table,
    parents,
    routes,
    norm_gain,
    router,
    gate_w,
    up_w,
    down_w,
):
    kv_count = lax.axis_size("kv")
    n = math.isqrt(lax.axis_size("wide") // 2)
    step_tok, steps, width = queries.shape
    rows = step_tok * steps
    heads = width // HD
    slots = cache_keys.shape[1]
    groups = lengths.shape[0]
    model = router.shape[0]
    units = gate_w.shape[2]
    cols = n * n * MOST
    block = n * MOST
    spans = [(heads + 1) // 2, heads // 2]
    per_span = lambda shape, dtype: [vmem(shape(count), dtype) for count in spans]
    dma = pltpu.SemaphoreType.DMA
    vmem = pltpu.VMEM
    sems = lambda stages: (dma((stages, max(n, 4))), dma((stages, max(n, 4))))
    in_vmem = pl.BlockSpec(memory_space=pltpu.VMEM)
    in_smem = pl.BlockSpec(memory_space=pltpu.SMEM)
    in_hbm = pl.BlockSpec(memory_space=pl.ANY)
    return pl.pallas_call(
        functools.partial(kernel, n, kv_count, heads),
        out_shape=jax.ShapeDtypeStruct(stream_in.shape, BF16),
        in_specs=[in_vmem] * 3
        + [in_hbm] * 2
        + [in_smem, in_vmem, in_smem, in_vmem]
        + [in_hbm] * 5,
        out_specs=in_vmem,
        scratch_shapes=[
            vmem((slots, BLK, HD), BF16),
            vmem((slots, BLK, HD), BF16),
            vmem((router.shape[1], model), BF16),
            vmem((2 * units, model), BF16),
            vmem((2 * units, model), BF16),
            vmem((kv_count, 2 * units, width), BF16),
            vmem((1, model), F32),
            dma((6 + kv_count,)),
            (dma((3,)), dma((3,))),
            vmem((rows, width), BF16),
            per_span(lambda k: (rows, k * HD), BF16),
            per_span(lambda k: (2, n, n, rows, k * HD), BF16),
            vmem((4, rows, 2 * HD), BF16),
            vmem((n, rows, routes.shape[2]), jnp.int32),
            sems(8),
            pltpu.SMEM((slots,), jnp.int32),
            pltpu.SMEM((slots,), jnp.int32),
            pltpu.SMEM((slots,), jnp.int32),
            pltpu.SMEM((groups,), jnp.int32),
            per_span(lambda k: (slots + 1, 4 * rows * k, 2 * HD), F32),
            per_span(lambda k: (2, n, n * k + 1, rows, HD), BF16),
            per_span(lambda k: (n, n * k + 1, rows, HD), BF16),
            per_span(lambda k: (n, n * k + 1, rows, HD), BF16),
            per_span(lambda k: (n, n * k + 1, rows, HD), BF16),
            per_span(lambda k: (n, k + 1, rows, HD), BF16),
            per_span(lambda k: (n, k + 1, rows, HD), BF16),
            sems(6),
            vmem((rows, width), BF16),
            vmem((n, kv_count, rows, width), BF16),
            (dma((3, kv_count * n)), dma((3, kv_count * n))),
            pltpu.SemaphoreType.REGULAR,
            vmem((2, n, block // 2, model), BF16),
            vmem((2, n, block // 2, model), BF16),
            (dma((2, n)), dma((2, n))),
            vmem((2, kv_count, n, block // 2, width), BF16),
            vmem((2, kv_count, n, block // 2, width), BF16),
            vmem((n, rows, width), BF16),
            vmem((n, rows, width), BF16),
            (dma((n,)), dma((n,))),
        ],
        compiler_params=pltpu.CompilerParams(collective_id=0, has_side_effects=True),
        name="layer",
    )(
        stream_in,
        queries,
        new_kv,
        cache_keys,
        cache_values,
        lengths,
        page_table,
        jnp.swapaxes(parents, 0, 1),
        routes.reshape(rows, routes.shape[2]),
        norm_gain,
        jnp.swapaxes(router, 0, 1),
        jnp.swapaxes(gate_w, 1, 2),
        jnp.swapaxes(up_w, 1, 2),
        down_w,
    )


def solution(mesh):
    return jax.shard_map(
        local,
        mesh=mesh,
        in_specs=(
            P("wide", None, "kv"),
            P("wide", None, "kv"),
            P("wide", None, None, "kv"),
            P("kv", "wide", None, None),
            P("kv", "wide", None, None),
            P(),
            P(),
            P(),
            P("wide", None, None),
            P(),
            P(),
            P("wide", None, "kv"),
            P("wide", None, "kv"),
            P("wide", "kv", None),
        ),
        out_specs=P("wide", None, "kv"),
        check_vma=False,
    )
```

```python
import functools
import math

import jax
import jax.numpy as jnp
from jax import lax
from jax.experimental import pallas as pl
from jax.experimental.pallas import tpu as pltpu
from jax.sharding import PartitionSpec as P

MESH = pl.DeviceIdType.MESH
HD = 128
BEAMS = 8
BLK = 128
MOST = 2
F32 = jnp.float32
BF16 = jnp.bfloat16


def far_first(n):
    order = sorted(range(1, n), key=lambda d: -min(d, n - d))
    return order


def near_first(n):
    return sorted(range(1, n), key=lambda d: min(d, n - d))


def rcopy(src, dst, send_sem, recv_sem, device):
    return pltpu.make_async_remote_copy(
        src_ref=src,
        dst_ref=dst,
        send_sem=send_sem,
        recv_sem=recv_sem,
        device_id=device,
        device_id_type=MESH,
    )


def dot(x, y):
    return jnp.dot(x, y, preferred_element_type=F32)


def iota(shape, axis):
    return lax.broadcasted_iota(jnp.int32, shape, axis)


def kernel(
    n,
    kv_count,
    heads,
    stream_ref,
    query_ref,
    newkv_ref,
    keys_hbm,
    values_hbm,
    lengths_ref,
    table_ref,
    parents_ref,
    routes_ref,
    gain_hbm,
    router_hbm,
    gate_hbm,
    up_hbm,
    down_hbm,
    out_ref,
    keys,
    values,
    router,
    gate,
    up,
    down,
    gain,
    load_sem,
    weight_sems,
    query,
    query_parts,
    q_all,
    kvgroup,
    routes_b,
    q_sems,
    slot_group,
    slot_limit,
    slot_prev,
    group_last,
    sums_all,
    part_all,
    sibling_part,
    core_sum_all,
    b_parts,
    b_sum,
    a_parts,
    part_sems,
    resid,
    mid_resid,
    x_sems,
    line_ready,
    mid_perm,
    rows,
    row_sems,
    x_send,
    back_mid,
    back_sum,
    back_rows,
    back_sems,
):
    kv = lax.axis_index("kv")
    w = lax.axis_index("wide")
    c = w % 2
    z = (w // 2) % n
    y = w // (2 * n)
    a = z + c * (y - z)
    b = y + c * (z - y)
    stride_a = 2 + c * (2 * n - 2)
    stride_b = 2 * n - c * (2 * n - 2)
    sib = {"wide": w + 1 - 2 * c}
    width = heads * HD
    row_count = query.shape[0]
    slots = keys.shape[0]
    groups = lengths_ref.shape[0]
    blocks = table_ref.shape[1]
    steps = parents_ref.shape[0] + 1
    top = routes_ref.shape[1]
    units = gate.shape[0] // 2
    w_send, w_recv = weight_sems
    model = kv_count * width
    cols = n * n * MOST
    block_rows = n * MOST
    mids = n * row_count
    half_cols = cols // 2
    half_rows = block_rows // 2
    scale = 1.0 / math.sqrt(HD)

    def dev_a(j):
        return {"wide": w + (j - a) * stride_a}

    def dev_b(j):
        return {"wide": w + (j - b) * stride_b}

    def dev_xa(i, j):
        return {"kv": i, "wide": w + (j - a) * stride_a}

    def dev_xb(i, j):
        return {"kv": i, "wide": w + (j - b) * stride_b}

    spans = [(0, (heads + 1) // 2), ((heads + 1) // 2, heads)]

    group_first = w // 4 * 4
    group_place = w % 4

    loads = [
        pltpu.make_async_copy(src, dst, load_sem.at[i])
        for i, (src, dst) in enumerate(
            [
                (keys_hbm.at[0], keys),
                (values_hbm.at[0], values),
                (router_hbm, router),
                (gate_hbm.at[0], gate.at[0:units]),
                (up_hbm.at[0], up.at[0:units]),
                (gain_hbm, gain.at[0]),
            ]
            + [
                (down_hbm.at[0, :, i * width : (i + 1) * width], down.at[i, 0:units])
                for i in range(kv_count)
            ]
        )
    ]
    query[...] = query_ref[...].reshape(query.shape)
    for (first, last), share_q, all_q in zip(spans, query_parts, q_all):
        share_q[...] = query[:, first * HD : last * HD]
        all_q[c, b, a] = share_q[...]
    kvgroup[group_place] = newkv_ref[...].reshape(row_count, 2 * HD)
    routes_b[b] = routes_ref[...]

    barrier = pltpu.get_barrier_semaphore()
    greeted = 0
    for d in far_first(n):
        for device in (dev_a((a + d) % n), dev_b((b + d) % n)):
            pl.semaphore_signal(barrier, inc=1, device_id=device, device_id_type=MESH)
            greeted += 1
    kv_peers = [{"kv": (kv + d) % kv_count} for d in range(1, kv_count)]
    for device in kv_peers:
        pl.semaphore_signal(barrier, inc=1, device_id=device, device_id_type=MESH)
        greeted += 1
    for d in range(1, 4):
        pl.semaphore_signal(
            barrier,
            inc=1,
            device_id={"wide": group_first + (group_place + d) % 4},
            device_id_type=MESH,
        )
        greeted += 1
    pl.semaphore_wait(barrier, greeted)

    sent = []

    def send(copy):
        copy.start()
        sent.append(copy)

    q_send, q_recv = q_sems
    for ch, share_q in enumerate(query_parts):
        for d in far_first(n):
            send(
                rcopy(
                    share_q,
                    q_all[ch].at[c, b, a],
                    q_send.at[7 * ch, d],
                    q_recv.at[7 * ch, a],
                    dev_a((a + d) % n),
                )
            )
    for load in loads[:2]:
        load.start()
    for device in kv_peers:
        pl.semaphore_signal(line_ready, inc=1, device_id=device, device_id_type=MESH)
    for d in range(1, 4):
        peer = group_first + (group_place + d) % 4
        send(
            rcopy(
                kvgroup.at[group_place],
                kvgroup.at[group_place],
                q_send.at[3, d],
                q_recv.at[3, group_place],
                {"wide": peer},
            )
        )

    for ch in range(2):
        for d in near_first(n):
            j = (a + d) % n
            rcopy(
                query_parts[ch], q_all[ch].at[c, b, j], q_send.at[7 * ch, d], q_recv.at[7 * ch, j], dev_a(j)
            ).wait_recv()
        block = q_all[ch].at[c, b]
        for d in near_first(n):
            send(
                rcopy(
                    block, block, q_send.at[1 + 4 * ch, d], q_recv.at[1 + 4 * ch, b], dev_b((b + d) % n)
                )
            )
        send(rcopy(block, block, q_send.at[2 + 4 * ch, 0], q_recv.at[2 + 4 * ch, b], sib))
    for d in far_first(n):
        send(
            rcopy(
                routes_b.at[b],
                routes_b.at[b],
                q_send.at[4, d],
                q_recv.at[4, b],
                dev_b((b + d) % n),
            )
        )

    for load in loads[2:]:
        load.start()

    table = table_ref[...]
    place = iota((groups, blocks), 0) * blocks + iota((groups, blocks), 1) + 1
    owners = []
    for s in range(slots):
        code = jnp.max(jnp.where(table == w * slots + s, place, 0))
        live = jnp.minimum(code, 1)
        spot = jnp.maximum(code - 1, 0)
        group = spot // blocks
        slot_group[s] = group
        slot_limit[s] = live * (lengths_ref[group] - spot % blocks * BLK)
        owners.append(jnp.where(code > 0, group, -1))
    for s in range(slots):
        before = jnp.int32(slots)
        for r in range(s):
            before = jnp.where(owners[r] == owners[s], r, before)
        slot_prev[s] = before
    for g in range(groups):
        last = jnp.int32(slots)
        for s in range(slots):
            last = jnp.where(owners[s] == g, s, last)
        group_last[g] = last

    def pass_on(ch):
        for d in near_first(n):
            j = (b + d) % n
            block = q_all[ch].at[c, j]
            rcopy(
                block, block, q_send.at[1 + 4 * ch, d], q_recv.at[1 + 4 * ch, j], dev_b(j)
            ).wait_recv()
            send(rcopy(block, block, q_send.at[2 + 4 * ch, d], q_recv.at[2 + 4 * ch, j], sib))

    def await_sibling(ch):
        for j in range(n):
            block = q_all[ch].at[1 - c, j]
            rcopy(
                block, block, q_send.at[2 + 4 * ch, j], q_recv.at[2 + 4 * ch, j], sib
            ).wait_recv()

    half_n = n // 2
    group_rows = 4 * row_count
    lane = iota((row_count, HD), 1)
    p_send, p_recv = part_sems

    def attend(ch):
        first_head, last_head = spans[ch]
        count = last_head - first_head
        sums, part = sums_all[ch], part_all[ch]
        tiles = n * count
        qfull = q_all[ch]

        def one_slot(s):
            group = slot_group[s]
            gy = group // half_n
            gz = group % half_n * 2
            q = jnp.concatenate(
                [
                    qfull[0, gy, gz],
                    qfull[0, gy, gz + 1],
                    qfull[1, gz, gy],
                    qfull[1, gz + 1, gy],
                ],
                axis=0,
            )
            q = jnp.concatenate([q[:, r * HD : (r + 1) * HD] for r in range(count)], axis=0)
            scores = lax.dot_general(
                q, keys[s], (((1,), (1,)), ((), ())), preferred_element_type=F32
            )
            ok = iota(scores.shape, 1) < slot_limit[s]
            weights = jnp.where(ok, jnp.exp(scores * scale), 0.0).astype(BF16)
            extended = jnp.concatenate([values[s], jnp.ones((BLK, HD), BF16)], axis=1)
            sums[s] = dot(weights, extended)

        def slot_block(s, carry):
            for i in range(4):
                one_slot(s * 4 + i)
            return carry

        sums[slots] = jnp.zeros(sums.shape[1:], F32)
        lax.fori_loop(0, slots // 4, slot_block, 0)

        def link_slot(s, carry):
            sums[s] = sums[s] + sums[slot_prev[s]]
            return carry

        lax.fori_loop(0, slots, link_slot, 0)

        for core in range(2):
            for j in range(n):
                part[core, j, tiles] = jnp.zeros((row_count, HD), BF16)

        def one_group(g, carry):
            last = group_last[g]
            gy = g // half_n
            gz = g % half_n * 2
            for core in range(2):
                for zl in range(2):
                    bi, ai = (gy, gz + zl) if core == 0 else (gz + zl, gy)
                    dens = jnp.zeros((row_count, HD), F32)
                    for r in range(count):
                        first = r * group_rows + (core * 2 + zl) * row_count
                        block = sums[last, pl.ds(first, row_count), :]
                        part[core, bi, ai * count + r] = block[:, :HD].astype(BF16)
                        dens = jnp.where(lane % 8 == r, block[:, HD:], dens)
                    old = part[core, bi, tiles].astype(F32)
                    part[core, bi, tiles] = jnp.where(lane // 8 == ai, dens, old).astype(BF16)
            return carry

        lax.fori_loop(0, groups, one_group, 0)
        for d in far_first(n) + [0]:
            j = (a + d) % n
            send(
                rcopy(
                    part.at[1 - c, j],
                    sibling_part[ch].at[j],
                    p_send.at[3 * ch, d],
                    p_recv.at[3 * ch, j],
                    sib,
                )
            )

    def sum_cores(ch):
        part, core_sum = part_all[ch], core_sum_all[ch]
        for d in near_first(n) + [0]:
            j = (b + d) % n
            rcopy(
                part.at[1 - c, j],
                sibling_part[ch].at[j],
                p_send.at[3 * ch, d],
                p_recv.at[3 * ch, j],
                sib,
            ).wait_recv()
            core_sum[j] = (part[c, j].astype(F32) + sibling_part[ch][j].astype(F32)).astype(BF16)
            if d:
                send(
                    rcopy(
                        core_sum.at[j],
                        b_parts[ch].at[b],
                        p_send.at[3 * ch + 1, d],
                        p_recv.at[3 * ch + 1, b],
                        dev_b(j),
                    )
                )

    for j in range(1, 4):
        p = (group_place + j) % 4
        rcopy(
            kvgroup.at[p], kvgroup.at[p], q_send.at[3, j], q_recv.at[3, p], {"wide": group_first + p}
        ).wait_recv()
    key_rows = 4 * row_count
    tail_kv = jnp.concatenate([kvgroup[i] for i in range(4)], axis=0)
    row_id = iota((row_count, key_rows), 0)
    key_id = iota((row_count, key_rows), 1)
    wanted = jnp.full((row_count, key_rows), -1, jnp.int32)
    token_base = w // 4 * BEAMS
    for i in range(row_count // steps):
        for s in range(steps):
            beam = group_place * (row_count // steps) + i
            for j in range(s, -1, -1):
                wanted = jnp.where(
                    (row_id == i * steps + s) & (key_id % steps == j), beam, wanted
                )
                if j:
                    beam = parents_ref[j - 1, token_base + beam]
    allowed = wanted == key_id // steps
    tail_q = jnp.concatenate([query[:, r * HD : (r + 1) * HD] for r in range(heads)], axis=0)
    tail_scores = lax.dot_general(
        tail_q, tail_kv[:, :HD], (((1,), (1,)), ((), ())), preferred_element_type=F32
    )
    tail_ok = jnp.concatenate([allowed.astype(F32)] * heads, axis=0)
    tail_w = jnp.where(tail_ok > 0, jnp.exp(tail_scores * scale), 0.0).astype(BF16)
    tail_num = dot(tail_w, tail_kv[:, HD:])
    tail_den = jnp.sum(tail_w.astype(F32), axis=1, keepdims=True)

    pass_on(0)
    await_sibling(0)
    loads[0].wait()
    loads[1].wait()
    attend(0)
    pass_on(1)
    sum_cores(0)
    await_sibling(1)
    attend(1)
    sum_cores(1)

    for load in loads[3:5] + loads[6:]:
        load.wait()
    halves = [(gate, 0), (up, 1), (down, 2)]
    for weight, i in halves:
        rows_of = (slice(None),) * (len(weight.shape) - 2)
        send(
            rcopy(
                weight.at[rows_of + (pl.ds(0, units),)],
                weight.at[rows_of + (pl.ds(units, units),)],
                w_send.at[i],
                w_recv.at[i],
                sib,
            )
        )

    for ch, (first_head, last_head) in enumerate(spans):
        count = last_head - first_head
        core_sum, part_b, sum_b = core_sum_all[ch], b_parts[ch], b_sum[ch]
        for d in near_first(n):
            j = (b + d) % n
            rcopy(
                core_sum.at[j], part_b.at[j], p_send.at[3 * ch + 1, d], p_recv.at[3 * ch + 1, j], dev_b(j)
            ).wait_recv()
        dens = core_sum[b, n * count].astype(F32)
        for e in range(1, n):
            dens = dens + part_b[(b + e) % n, n * count].astype(F32)
        dens = dens.astype(BF16)
        for d in far_first(n) + [0]:
            j = (a + d) % n
            chunk = pl.ds(j * count, count)
            total = core_sum[b, chunk].astype(F32)
            for e in range(1, n):
                total = total + part_b[(b + e) % n, chunk].astype(F32)
            sum_b[j, 0:count] = total.astype(BF16)
            sum_b[j, count] = dens
            if d:
                send(
                    rcopy(
                        sum_b.at[j],
                        a_parts[ch].at[a],
                        p_send.at[3 * ch + 2, d],
                        p_recv.at[3 * ch + 2, a],
                        dev_a(j),
                    )
                )
    nums = []
    dens = []
    for ch, (first_head, last_head) in enumerate(spans):
        count = last_head - first_head
        total = b_sum[ch][a].astype(F32)
        for d in near_first(n):
            j = (a + d) % n
            rcopy(
                b_sum[ch].at[j], a_parts[ch].at[j], p_send.at[3 * ch + 2, d], p_recv.at[3 * ch + 2, j], dev_a(j)
            ).wait_recv()
            total = total + a_parts[ch][j].astype(F32)
        for r in range(count):
            nums.append(total[r])
            mine = jnp.where(lane == a * 8 + r, total[count], 0.0)
            dens.append(jnp.sum(mine, axis=1, keepdims=True))

    attended = []
    for r in range(heads):
        num = nums[r] + tail_num[r * row_count : (r + 1) * row_count]
        den = dens[r] + tail_den[r * row_count : (r + 1) * row_count]
        attended.append((num / den).astype(BF16).astype(F32))
    residual = (stream_ref[...].reshape(row_count, width).astype(F32) + jnp.concatenate(attended, axis=1)).astype(BF16)
    resid[...] = residual

    x_ssem, x_rsem = x_sems
    pl.semaphore_wait(line_ready, kv_count - 1)
    spots = [(dx, d) for d in far_first(n) + [0] for dx in far_first(kv_count) + [0]]
    for dx, d in spots[:-1]:
        device = dev_xb((kv + dx) % kv_count, (b + d) % n)
        send(
            rcopy(
                resid,
                mid_resid.at[b, kv],
                x_ssem.at[0, dx * n + d],
                x_rsem.at[0, kv * n + b],
                device,
            )
        )
    mid_resid[b, kv] = residual
    for d in near_first(n):
        j = (b + d) % n
        rcopy(
            routes_b.at[j], routes_b.at[j], q_send.at[4, d], q_recv.at[4, j], dev_b(j)
        ).wait_recv()
    routed = jnp.concatenate([routes_b[(b + p) % n] for p in range(n)], axis=0)
    col = iota((1, cols), 1)
    col_chip = col % half_cols // half_rows
    col_source = col // half_cols * half_n + col // MOST % half_n
    col_place = col % MOST
    col_expert = b * n + col_chip + c * ((col_chip - b) * (n - 1))
    experts = n * n
    source = iota((mids, 1), 0) // row_count
    expert_lane = iota((1, experts), 1)
    hit = jnp.zeros((mids, cols), F32)
    chosen = jnp.zeros((mids, experts), F32)
    for i in range(top):
        hit = jnp.where(routed[:, i : i + 1] == col_expert, 1.0, hit)
        chosen = jnp.where(routed[:, i : i + 1] == expert_lane, 1.0, chosen)
    hit = jnp.where(source == col_source, hit, 0.0)
    first_id = iota((mids, mids), 0)
    second_id = iota((mids, mids), 1)
    earlier = (first_id > second_id) & (first_id // row_count == second_id // row_count)
    taken = dot(earlier.astype(F32).astype(BF16), hit.astype(BF16))
    pick = jnp.where(taken == col_place.astype(F32), hit, 0.0)
    pick_t = jnp.transpose(pick).astype(BF16)
    spread = (iota((experts, cols), 0) == col_expert).astype(F32)

    loads[2].wait()
    loads[5].wait()
    for dx, d in reversed(spots[:-1]):
        i, j = (kv + dx) % kv_count, (b + d) % n
        rcopy(
            resid, mid_resid.at[j, i], x_ssem.at[0, dx * n + d], x_rsem.at[0, i * n + j], dev_xb(i, j)
        ).wait_recv()
    full = jnp.concatenate(
        [
            jnp.concatenate([mid_resid[(b + p) % n, i] for p in range(n)], axis=0).astype(F32)
            for i in range(kv_count)
        ],
        axis=1,
    )
    mean_square = jnp.sum(full * full, axis=1, keepdims=True) / model
    mid = (full * lax.rsqrt(mean_square + 1e-06) * gain[...]).astype(BF16)

    r_send, r_recv = row_sems
    for u in (1, 0):
        picked = dot(pick_t[u * half_cols : (u + 1) * half_cols], mid)
        mid_perm[u] = picked.astype(BF16).reshape(mid_perm.shape[1:])
        for d in far_first(n):
            j = (a + d) % n
            send(
                rcopy(mid_perm.at[u, j], rows.at[u, a], r_send.at[u, d], r_recv.at[u, a], dev_a(j))
            )
        rows[u, a] = mid_perm[u, a]

    logits = lax.dot_general(
        mid, router[...], (((1,), (1,)), ((), ())), preferred_element_type=F32
    )
    col_logits = lax.dot_general(
        logits,
        spread,
        (((1,), (0,)), ((), ())),
        preferred_element_type=F32,
        precision=lax.Precision.HIGHEST,
    )
    raised = jnp.where(chosen > 0, jnp.exp(jnp.where(chosen > 0, logits, 0.0)), 0.0)
    raised_sum = jnp.sum(raised, axis=1, keepdims=True)
    share = jnp.where(pick > 0, jnp.exp(jnp.where(pick > 0, col_logits, 0.0)), 0.0) / raised_sum
    share_high = share.astype(BF16)
    share_low = (share - share_high.astype(F32)).astype(BF16)

    for weight, i in halves:
        rows_of = (slice(None),) * (len(weight.shape) - 2)
        half = weight.at[rows_of + (pl.ds(units, units),)]
        rcopy(half, half, w_send.at[i], w_recv.at[i], sib).wait_recv()
    turned = (((1,), (1,)), ((), ()))
    for u in (1, 0):
        for d in near_first(n):
            j = (a + d) % n
            rcopy(
                mid_perm.at[u, j], rows.at[u, j], r_send.at[u, d], r_recv.at[u, j], dev_a(j)
            ).wait_recv()
        x = rows[u].reshape(half_cols, model)
        gated = lax.dot_general(x, gate[...], turned, preferred_element_type=F32)
        lifted = lax.dot_general(x, up[...], turned, preferred_element_type=F32)
        hidden = (gated / (1.0 + jnp.exp(-gated)) * lifted).astype(BF16)
        for d in far_first(kv_count) + [0]:
            i = (kv + d) % kv_count
            x_send[u, i] = dot(hidden, down[i]).astype(BF16).reshape(x_send.shape[2:])
            for da in far_first(n) + [0]:
                j = (a + da) % n
                if d or da:
                    send(
                        rcopy(
                            x_send.at[u, i, j],
                            back_mid.at[u, kv, a],
                            x_ssem.at[1 + u, d * n + da],
                            x_rsem.at[1 + u, kv * n + a],
                            dev_xa(i, j),
                        )
                    )
        back_mid[u, kv, a] = x_send[u, kv, a]

    e_send, e_recv = back_sems
    half_mids = mids // 2
    for u in (1, 0):
        own_rows = slice(u * half_mids, (u + 1) * half_mids)
        own_cols = slice(u * half_cols, (u + 1) * half_cols)
        shares = [
            jnp.concatenate([part[own_rows, own_cols]] * kv_count, axis=1)
            for part in (share_high, share_low)
        ]
        for dx, d in [(dx, d) for d in [0] + near_first(n) for dx in range(kv_count)][1:]:
            i, j = (kv + dx) % kv_count, (a + d) % n
            rcopy(
                x_send.at[u, i, j],
                back_mid.at[u, i, j],
                x_ssem.at[1 + u, dx * n + d],
                x_rsem.at[1 + u, i * n + j],
                dev_xa(i, j),
            ).wait_recv()
        returned = back_mid[u].reshape(kv_count * half_cols, width)
        weighted = dot(shares[0], returned) + dot(shares[1], returned)
        back_sum[u * half_n : (u + 1) * half_n] = weighted.astype(BF16).reshape((half_n,) + back_sum.shape[1:])
        for p in far_first(n):
            if p // half_n == u:
                send(
                    rcopy(
                        back_sum.at[p], back_rows.at[b], e_send.at[p], e_recv.at[b], dev_b((b + p) % n)
                    )
                )
    combined = resid[...].astype(F32) + back_sum[0].astype(F32)
    for d in near_first(n):
        j = (b + d) % n
        rcopy(
            back_sum.at[d], back_rows.at[j], e_send.at[d], e_recv.at[j], dev_b(j)
        ).wait_recv()
        combined = combined + back_rows[j].astype(F32)
    out_ref[...] = combined.astype(BF16).reshape(out_ref.shape)
    for copy in sent:
        copy.wait_send()


def local(
    stream_in,
    queries,
    new_kv,
    cache_keys,
    cache_values,
    lengths,
    page_table,
    parents,
    routes,
    norm_gain,
    router,
    gate_w,
    up_w,
    down_w,
):
    kv_count = lax.axis_size("kv")
    n = math.isqrt(lax.axis_size("wide") // 2)
    step_tok, steps, width = queries.shape
    rows = step_tok * steps
    heads = width // HD
    slots = cache_keys.shape[1]
    groups = lengths.shape[0]
    model = router.shape[0]
    units = gate_w.shape[2]
    cols = n * n * MOST
    block = n * MOST
    spans = [(heads + 1) // 2, heads // 2]
    per_span = lambda shape, dtype: [vmem(shape(count), dtype) for count in spans]
    dma = pltpu.SemaphoreType.DMA
    vmem = pltpu.VMEM
    sems = lambda stages: (dma((stages, max(n, 4))), dma((stages, max(n, 4))))
    in_vmem = pl.BlockSpec(memory_space=pltpu.VMEM)
    in_smem = pl.BlockSpec(memory_space=pltpu.SMEM)
    in_hbm = pl.BlockSpec(memory_space=pl.ANY)
    return pl.pallas_call(
        functools.partial(kernel, n, kv_count, heads),
        out_shape=jax.ShapeDtypeStruct(stream_in.shape, BF16),
        in_specs=[in_vmem] * 3
        + [in_hbm] * 2
        + [in_smem, in_vmem, in_smem, in_vmem]
        + [in_hbm] * 5,
        out_specs=in_vmem,
        scratch_shapes=[
            vmem((slots, BLK, HD), BF16),
            vmem((slots, BLK, HD), BF16),
            vmem((router.shape[1], model), BF16),
            vmem((2 * units, model), BF16),
            vmem((2 * units, model), BF16),
            vmem((kv_count, 2 * units, width), BF16),
            vmem((1, model), F32),
            dma((6 + kv_count,)),
            (dma((3,)), dma((3,))),
            vmem((rows, width), BF16),
            per_span(lambda k: (rows, k * HD), BF16),
            per_span(lambda k: (2, n, n, rows, k * HD), BF16),
            vmem((4, rows, 2 * HD), BF16),
            vmem((n, rows, routes.shape[2]), jnp.int32),
            sems(8),
            pltpu.SMEM((slots,), jnp.int32),
            pltpu.SMEM((slots,), jnp.int32),
            pltpu.SMEM((slots,), jnp.int32),
            pltpu.SMEM((groups,), jnp.int32),
            per_span(lambda k: (slots + 1, 4 * rows * k, 2 * HD), F32),
            per_span(lambda k: (2, n, n * k + 1, rows, HD), BF16),
            per_span(lambda k: (n, n * k + 1, rows, HD), BF16),
            per_span(lambda k: (n, n * k + 1, rows, HD), BF16),
            per_span(lambda k: (n, n * k + 1, rows, HD), BF16),
            per_span(lambda k: (n, k + 1, rows, HD), BF16),
            per_span(lambda k: (n, k + 1, rows, HD), BF16),
            sems(6),
            vmem((rows, width), BF16),
            vmem((n, kv_count, rows, width), BF16),
            (dma((3, kv_count * n)), dma((3, kv_count * n))),
            pltpu.SemaphoreType.REGULAR,
            vmem((2, n, block // 2, model), BF16),
            vmem((2, n, block // 2, model), BF16),
            (dma((2, n)), dma((2, n))),
            vmem((2, kv_count, n, block // 2, width), BF16),
            vmem((2, kv_count, n, block // 2, width), BF16),
            vmem((n, rows, width), BF16),
            vmem((n, rows, width), BF16),
            (dma((n,)), dma((n,))),
        ],
        compiler_params=pltpu.CompilerParams(collective_id=0, has_side_effects=True),
        name="layer",
    )(
        stream_in,
        queries,
        new_kv,
        cache_keys,
        cache_values,
        lengths,
        page_table,
        jnp.swapaxes(parents, 0, 1),
        routes.reshape(rows, routes.shape[2]),
        norm_gain,
        jnp.swapaxes(router, 0, 1),
        jnp.swapaxes(gate_w, 1, 2),
        jnp.swapaxes(up_w, 1, 2),
        down_w,
    )


def solution(mesh):
    return jax.shard_map(
        local,
        mesh=mesh,
        in_specs=(
            P("wide", None, "kv"),
            P("wide", None, "kv"),
            P("wide", None, None, "kv"),
            P("kv", "wide", None, None),
            P("kv", "wide", None, None),
            P(),
            P(),
            P(),
            P("wide", None, None),
            P(),
            P(),
            P("wide", None, "kv"),
            P("wide", None, "kv"),
            P("wide", "kv", None),
        ),
        out_specs=P("wide", None, "kv"),
        check_vma=False,
    )
```
